32 devices in a mesh: row: 4 (over y, x), col: 8 (over z, core).
Axes of the slice: x: 2, y: 2, z: 4, core: 2. Of those that a mesh axis runs over, the one named last changes fastest.
Arguments:
- targets: float32 [2, 16384], P(None, ('row', 'col')), may hold values from 0 to 1
- sources: bfloat16 [2, 16384], P(None, 'col'), may hold values from 0 to 1
- omega: bfloat16 [256, 16384], P(None, 'col'), may hold values from -0.046875 to 0.046875
- tree_order: int32 [16384], P(('row', 'col')), may hold values from 0 to 16383, each once
- leaf_pivots: int32 [32, 128], P(('row', 'col')), may hold values from 0 to 511, all different within a row
- pivots_one: int32 [16, 128], replicated, may hold values from 0 to 255, all different within a row
- pivots_two: int32 [8, 128], replicated, may hold values from 0 to 255, all different within a row
- pivots_three: int32 [4, 128], replicated, may hold values from 0 to 255, all different within a row
Outputs:
- leaf_interp: float32 [16384, 128], P(('row', 'col'))
- level_one_interp: float32 [4096, 128], P(('row', 'col'))
- level_two_interp: float32 [2048, 128], P(('row', 'col'))
- level_three_interp: float32 [1024, 128], P(('row', 'col'))
- root_sketch: float32 [512, 256], P(('row', 'col'))
The draws below stay inside these ranges and needn't reach their ends.
Inputs may be any that keep to these rules, and one draw needn't show every extreme that they name: tree_order names every target point once. `leaf_pivots`: each row names 128 distinct positions. `pivots_one`: each row names 128 distinct positions. `pivots_two`: each row names 128 distinct positions. `pivots_three`: each row names 128 distinct positions.
All inputs are finite; a program needn't handle non-finite values.
Results may differ from the reference program's by a relative error of at most 0.0074.
Values may be sent and summed in bfloat16 or wider, within the bound.
A program may use at most 192 MiB of HBM per device.

```python
import jax
import jax.numpy as jnp
from jax import lax

LEAF = 512
K = 128
S = 256
N = 16384
P_SIZE = 16384
NODES1 = 16
NODES2 = 8
NODES3 = 4


def level_of(own_key, extent, cuts, low, largest):
    def one(dim, blocks):
        heights = jax.random.uniform(jax.random.fold_in(jax.random.fold_in(own_key, 6), dim), (blocks,), jnp.float32, low / len(cuts), largest / len(cuts))
        return jnp.repeat(jnp.exp(heights), extent[dim] // blocks).reshape((-1,) + (1,) * (len(extent) - dim - 1))

    loudness = one(*cuts[0])
    for cut in cuts[1:]:
        loudness = loudness * one(*cut)
    return loudness


def choose_distinct(stream_key, rows, amount, top, lift):
    ranking = jax.random.permutation(jax.random.fold_in(stream_key, 1), amount)
    favour = ranking
    for power in range(3):
        favour = favour * favour // amount
    favour = favour * lift // amount
    chance = jax.random.randint(jax.random.fold_in(stream_key, 2), (rows, amount), 0, 4096) + favour
    sure = jax.random.permutation(jax.random.fold_in(stream_key, 3), rows)[jnp.arange(amount) % rows]
    chance = jnp.where(jnp.arange(rows)[:, None] == sure[None, :], 1 << 14, chance)
    priority = chance * amount + jnp.arange(amount)
    return lax.top_k(priority.astype(jnp.int32), top)[1].astype(jnp.int32)


def bell_draw(stream_key, dims, deviation, bound, cuts=(), held_as=jnp.bfloat16):
    array = jax.random.normal(stream_key, dims, jnp.float32) * deviation
    if len(cuts) > 0:
        array = level_of(stream_key, dims, cuts, -0.22, 0.18) * array
    return jnp.clip(array, min=-bound, max=bound).astype(held_as)


def setup_inputs(seed: int = 0) -> dict:
    key_of = jax.random.split(jax.random.key(seed), 9)
    targets = jnp.clip(1.0 * jax.random.uniform(key_of[0], (2, N), jnp.float32) ** level_of(key_of[0], (2, N), ((1, 32),), -0.2, 0.2), 0.0, 1.0)
    sources = jnp.clip(1.0 * jax.random.uniform(key_of[1], (2, P_SIZE), jnp.float32) ** level_of(key_of[1], (2, P_SIZE), ((1, 8),), -0.2, 0.2), 0.0, 1.0).astype(jnp.bfloat16)
    omega = bell_draw(key_of[2], (S, P_SIZE), P_SIZE ** -0.5, 0.046875, ((1, 8),))
    tree_order = jax.random.permutation(key_of[3], N).astype(jnp.int32)
    leaf_pivots = choose_distinct(key_of[4], (N // LEAF), LEAF, K, 0)
    pivots_one = choose_distinct(key_of[5], NODES1, 2 * K, K, 0)
    pivots_two = choose_distinct(key_of[6], NODES2, 2 * K, K, 0)
    pivots_three = choose_distinct(key_of[7], NODES3, 2 * K, K, 0)
    return {"targets": targets, "sources": sources, "omega": omega, "tree_order": tree_order, "leaf_pivots": leaf_pivots, "pivots_one": pivots_one, "pivots_two": pivots_two, "pivots_three": pivots_three}


RIDGE = 0.1
DELTA_SQUARED = 0.0001

def kernel_block(points, source_pts):
    delta_x = points[0][:, None] - source_pts[0][None, :].astype(jnp.float32)
    delta_y = points[1][:, None] - source_pts[1][None, :].astype(jnp.float32)
    return (-0.5 * jnp.log(delta_x * delta_x + delta_y * delta_y + DELTA_SQUARED)).astype(jnp.bfloat16)

def select_factor(candidates, pivots):
    chosen = jnp.take(candidates, pivots, axis=0)
    gram_matrix = jnp.dot(chosen, chosen.T, precision=lax.Precision.HIGHEST)
    ridge_shift = RIDGE * (jnp.trace(gram_matrix) / chosen.shape[0] + 1e-06)
    shifted = gram_matrix + ridge_shift * jnp.eye(chosen.shape[0], dtype=gram_matrix.dtype)
    return (chosen, jnp.linalg.cholesky(shifted))

def solve_rows(chosen, factor, row_block):
    right_side = jnp.dot(chosen, row_block.T, precision=lax.Precision.HIGHEST)
    first = lax.linalg.triangular_solve(factor, right_side, left_side=True, lower=True)
    second = lax.linalg.triangular_solve(factor, first, left_side=True, lower=True, transpose_a=True)
    return second.T

def reference(targets, sources, omega, tree_order, leaf_pivots, pivots_one, pivots_two, pivots_three):
    placed = jnp.take(targets, tree_order, axis=1)
    blocks = placed.reshape(2, N // LEAF, LEAF).transpose(1, 0, 2)

    def sketch_block(block):
        panel = kernel_block(block, sources)
        return lax.dot_general(panel.astype(jnp.float32), omega.astype(jnp.float32), (((1,), (1,)), ((), ())), preferred_element_type=jnp.float32)
    leaf_sketches = lax.map(sketch_block, blocks)
    chosen, factors = jax.vmap(select_factor)(leaf_sketches, leaf_pivots)
    results = [jax.vmap(solve_rows)(chosen, factors, leaf_sketches).reshape(N, K)]
    for pivot_table in (pivots_one, pivots_two, pivots_three):
        candidates = chosen.reshape(-1, 2 * K, S)
        chosen, factors = jax.vmap(select_factor)(candidates, pivot_table)
        results.append(jax.vmap(solve_rows)(chosen, factors, candidates).reshape(-1, K))
    return (results[0], results[1], results[2], results[3], chosen.reshape(-1, S))
```

```python
import functools

import jax
import jax.numpy as jnp
from jax import lax
from jax.experimental import pallas as pl
from jax.experimental.pallas import tpu as pltpu
from jax.sharding import PartitionSpec as P

RIDGE = 0.1
DELTA_SQUARED = 0.0001
LEVELS = 3
LANES = 128
CHUNK = 512
SIDE = 24
LN2 = 0.6931471805599453
MESH = pl.DeviceIdType.MESH
HIGHEST = lax.Precision.HIGHEST
F32 = jnp.float32
BF16 = jnp.bfloat16


def split3(x):
    a = x.astype(BF16)
    r = x - a.astype(F32)
    b = r.astype(BF16)
    c = (r - b.astype(F32)).astype(BF16)
    return a, b, c


def pick_columns(pieces, pivots):
    m = pieces[0].shape[1]
    hot = (
        lax.broadcasted_iota(jnp.int32, (m, pivots.shape[1]), 0) == pivots
    ).astype(F32).astype(BF16)
    out = None
    for piece in pieces:
        term = jnp.dot(piece, hot, preferred_element_type=F32)
        out = term if out is None else out + term
    return out


def flip(value, mask, bits):
    out = 0
    for i in range(bits):
        out = out + (value // 2**i + mask // 2**i) % 2 * 2**i
    return out


def sketch_kernel(
    rows, cols,
    tgt_hbm, src_hbm, om_hbm, ord_hbm, leaf_hbm, p1_hbm, p2_hbm, p3_hbm,
    sk_ref, ch_ref, inv_ref,
    src_ref, om_ref, leaf_ref, p1_ref, p2_ref, p3_ref,
    every, orders, table, src_left, acc, part_out, part_in, z_out, z_in, ex_out, ex_in,
    load_sem,
    tgt_send, tgt_recv, ord_send, ord_recv, part_send, part_recv, z_send, z_recv,
    ex_send, ex_recv, pass_send, pass_recv,
):
    n = rows * cols
    zs = cols // 2
    bits = zs.bit_length() - 1
    row = lax.axis_index("row")
    col = lax.axis_index("col")
    me = row * cols + col
    z = col // 2
    core = col % 2
    partner = z * 2 + (1 - core)
    length = ord_hbm.shape[1]
    local = tgt_hbm.shape[1]
    per = 2 * local // LANES

    loads = [
        pltpu.make_async_copy(src, dst, load_sem.at[i])
        for i, (src, dst) in enumerate(
            (
                (src_hbm, src_ref), (om_hbm, om_ref), (leaf_hbm, leaf_ref),
                (p1_hbm, p1_ref), (p2_hbm, p2_ref), (p3_hbm, p3_ref),
                (tgt_hbm, every.at[me]), (ord_hbm, orders.at[col]),
            )
        )
    ]
    for load in loads:
        load.start()

    barrier = pltpu.get_barrier_semaphore()

    def greet(i, carry):
        other = lax.rem(me + i, n)
        pl.semaphore_signal(
            barrier, inc=1, device_id=(other // cols, other % cols), device_id_type=MESH
        )
        return carry

    lax.fori_loop(1, n, greet, 0)
    pl.semaphore_wait(barrier, n - 1)

    def tgt_copy(i):
        other = lax.rem(me + i, n)
        return pltpu.make_async_remote_copy(
            src_ref=tgt_hbm, dst_ref=every.at[me],
            send_sem=tgt_send.at[i], recv_sem=tgt_recv.at[i],
            device_id=(other // cols, other % cols), device_id_type=MESH,
        )

    def ord_copy(i):
        other = lax.rem(col + i, cols)
        return pltpu.make_async_remote_copy(
            src_ref=ord_hbm, dst_ref=orders.at[col],
            send_sem=ord_send.at[i], recv_sem=ord_recv.at[i],
            device_id=(row, other), device_id_type=MESH,
        )

    def start(copy):
        def go(i, carry):
            copy(i).start()
            return carry
        return go

    def finish(copy):
        def go(i, carry):
            copy(i).wait()
            return carry
        return go

    lax.fori_loop(1, n, start(tgt_copy), 0)
    lax.fori_loop(1, cols, start(ord_copy), 0)
    for load in loads:
        load.wait()

    def pieces(x):
        return [p.astype(F32) for p in split3(x)]

    wide = src_ref[...].astype(F32) - 0.5
    sx, sy = wide[0:1], wide[1:2]
    ones = jnp.ones_like(sx)
    left = []
    for part in (-2.0 * sx, -2.0 * sy):
        a, b, c = pieces(part)
        left += [a, a, a, b, b, c]
    left += pieces(sx * sx + sy * sy) + [ones] * 3
    left += [jnp.zeros_like(sx)] * (SIDE - len(left))
    src_left[...] = jnp.concatenate(left, axis=0).T.astype(BF16)

    lax.fori_loop(1, n, finish(tgt_copy), 0)
    lax.fori_loop(1, cols, finish(ord_copy), 0)

    flat = jnp.concatenate(
        [
            every[:, c, a * LANES : (a + 1) * LANES]
            for a in range(local // LANES)
            for c in range(2)
        ],
        axis=0,
    ).T
    for i, piece in enumerate(split3(flat)):
        table[i] = piece

    def points_of(leaf):
        order = orders[leaf]
        owner_row = order // LANES % (local // LANES) * (2 * n) + order // local
        lane = order % LANES
        rows_iota = lax.broadcasted_iota(jnp.int32, (n * per, length), 0)
        lane_iota = lax.broadcasted_iota(jnp.int32, (LANES, length), 0)
        out = []
        for c in range(2):
            hot = (rows_iota == owner_row + c * n).astype(F32).astype(BF16)
            got = jnp.dot(table[0], hot, preferred_element_type=F32)
            got += jnp.dot(table[1], hot, preferred_element_type=F32)
            got += jnp.dot(table[2], hot, preferred_element_type=F32)
            out.append(jnp.sum(jnp.where(lane_iota == lane, got, 0.0), axis=0, keepdims=True))
        return out

    sources = src_ref.shape[1]

    def block(leaf):
        px, py = points_of(leaf)
        px, py = px - 0.5, py - 0.5
        right = []
        for part in (px, py):
            a, b, c = pieces(part)
            right += [a, b, c, a, b, a]
        right += [jnp.ones_like(px)] * 3 + pieces(px * px + py * py + DELTA_SQUARED)
        right += [jnp.zeros_like(px)] * (SIDE - len(right))
        points = jnp.concatenate(right, axis=0).astype(BF16)

        def squares(at):
            return jnp.dot(
                src_left[at : at + CHUNK, :], points, preferred_element_type=F32
            )

        total = None
        ahead = squares(0)
        for at in range(0, sources, CHUNK):
            now = ahead
            if at + CHUNK < sources:
                ahead = squares(at + CHUNK)
            panel = ((-0.5 * LN2) * jnp.log2(now)).astype(BF16)
            term = jnp.dot(
                om_ref[:, at : at + CHUNK], panel, preferred_element_type=F32
            )
            total = term if total is None else total + term
        acc[...] = total

    def part_copy(x):
        return pltpu.make_async_remote_copy(
            src_ref=part_out.at[x], dst_ref=part_in.at[x],
            send_sem=part_send.at[x], recv_sem=part_recv.at[x],
            device_id=(row, partner), device_id_type=MESH,
        )

    def z_copy(x, b):
        return pltpu.make_async_remote_copy(
            src_ref=z_out.at[x], dst_ref=z_in.at[x],
            send_sem=z_send.at[x], recv_sem=z_recv.at[x],
            device_id=(row, flip(z, 2**b, bits) * 2 + core), device_id_type=MESH,
        )

    def both(x, received):
        to = flip(z, x, bits)
        block(to * 2 + (1 - core))
        part_out[x] = acc[...]
        part_copy(x).start()
        block(to * 2 + core)
        part_copy(x).wait()
        total = acc[...] + part_in[x]
        for b in range(received):
            z_copy(x + 2**b, b).wait()
            total = total + z_in[x + 2**b].astype(F32)
        return total

    for b in range(bits):
        count = zs // 2 ** (b + 1)

        def stage(j, carry, b=b, count=count):
            x = (2 * (count - 1 - j) + 1) * 2**b
            z_out[x] = both(x, b).astype(BF16)
            z_copy(x, b).start()
            return carry

        lax.fori_loop(0, count, stage, 0)
    sketch = both(0, bits)
    sk_ref[...] = sketch
    chosen = pick_columns(split3(sketch), leaf_ref[...])
    ch_ref[0] = chosen
    half = chosen.shape[0] // 2
    mine = pl.ds(pl.multiple_of(core * half, half), half)
    for s, p_ref in enumerate((p1_ref, p2_ref, p3_ref)):
        bit = col // 2**s % 2
        other = col + (1 - 2 * bit) * 2**s
        ex_out[s] = chosen
        if s == 0:
            copy = pltpu.make_async_remote_copy(
                src_ref=ex_out.at[s], dst_ref=ex_in.at[s],
                send_sem=ex_send.at[s], recv_sem=ex_recv.at[s],
                device_id=(row, other), device_id_type=MESH,
            )
            copy.start()
        else:
            copy = pltpu.make_async_remote_copy(
                src_ref=ex_out.at[s, mine], dst_ref=ex_in.at[s, mine],
                send_sem=ex_send.at[s], recv_sem=ex_recv.at[s],
                device_id=(row, other), device_id_type=MESH,
            )
            copy.start()
        if s == LEVELS - 1:
            inverse = shifted_inverses(
                [contract0(ch_ref[m], ch_ref[m]) for m in range(LEVELS)]
            )
            for m in range(LEVELS):
                inv_ref[m] = inverse[m]
        copy.wait()
        if s > 0:
            relay = pltpu.make_async_remote_copy(
                src_ref=ex_in.at[s, mine], dst_ref=ex_in.at[s, mine],
                send_sem=pass_send.at[s], recv_sem=pass_recv.at[s],
                device_id=(row, partner), device_id_type=MESH,
            )
            relay.start()
            relay.wait()
        theirs = ex_in[s]
        high = bit == 1
        low_part = jnp.where(high, theirs, chosen)
        high_part = jnp.where(high, chosen, theirs)
        cand = jnp.concatenate([low_part, high_part], axis=1)
        chosen = pick_columns(split3(cand), p_ref[pl.ds(me // 2 ** (s + 1), 1), :])
        ch_ref[s + 1] = chosen


def contract0(a, b):
    return lax.dot_general(
        a, b, (((0,), (0,)), ((), ())), precision=HIGHEST, preferred_element_type=F32
    )


def halves(x):
    h = x.astype(BF16)
    return h, (x - h.astype(F32)).astype(BF16)


def product3(a, b):
    ah, al = halves(a)
    bh, bl = halves(b)
    dot = functools.partial(jnp.dot, preferred_element_type=F32)
    return dot(ah, bh) + (dot(ah, bl) + dot(al, bh))


def product6(a, b):
    return jnp.dot(a, b, precision=HIGHEST, preferred_element_type=F32)


def shifted_inverses(grams):
    k = grams[0].shape[0]
    eye = lax.broadcasted_iota(jnp.int32, (k, k), 0) == lax.broadcasted_iota(
        jnp.int32, (k, k), 1
    )
    one = jnp.where(eye, 1.0, 0.0)
    low = 1.0 / (k / RIDGE + 1.0)
    gap = (1.0 - low) / (1.0 + low)
    first = 2.0 / (1.0 + low)
    tops, mats = [], []
    for gram in grams:
        trace = jnp.sum(jnp.where(eye, gram, 0.0), axis=(0, 1), keepdims=True)
        shift = RIDGE * (trace / k + 1e-06)
        tops.append(trace + shift)
        mats.append((gram + shift * one) / (trace + shift))
    scale = 2.0 / (2.0 - gap * gap)
    xs = [scale * (2.0 * first * one - first * first * m) for m in mats]
    gap = gap * gap / (2.0 - gap * gap)
    scales = []
    while gap > 1e-9:
        scales.append(2.0 / (2.0 - gap * gap))
        gap = gap * gap / (2.0 - gap * gap)
    for i, scale in enumerate(scales):
        product = product6 if i >= len(scales) - 2 else product3
        ys = [scale * (2.0 * one - product(m, x)) for m, x in zip(mats, xs)]
        xs = [product(x, y) for x, y in zip(xs, ys)]
    return [x / t for x, t in zip(xs, tops)]


def solve_kernel(sk_ref, ch_ref, inv_ref, o0, o1, o2, o3, root, r_ref, t_ref):
    col = lax.axis_index("col")
    levels = ch_ref.shape[0]
    top = ch_ref[levels - 1]
    inverse = [inv_ref[m] for m in range(levels - 1)] + shifted_inverses([contract0(top, top)])
    o0[...] = product6(contract0(sk_ref[...], ch_ref[0]), inverse[0])
    for s, o in enumerate((o1, o2, o3)):
        r_ref[...] = contract0(ch_ref[s], ch_ref[s + 1])
        size = o.shape[0]
        at = pl.multiple_of(col % 2**s * size, size)
        o[...] = product6(r_ref[pl.ds(at, size), :], inverse[s + 1])
    t_ref[...] = ch_ref[levels - 1].T
    size = root.shape[0]
    root[...] = t_ref[pl.ds(pl.multiple_of(col % 2**LEVELS * size, size), size), :]


def body(rows, cols, targets, sources, omega, tree_order, leaf_pivots, p1, p2, p3):
    n = rows * cols
    zs = cols // 2
    leaf = tree_order.shape[0]
    width = omega.shape[0]
    k = leaf_pivots.shape[1]
    per = targets.size // LANES
    vmem = pl.BlockSpec(memory_space=pltpu.VMEM)
    hbm = pl.BlockSpec(memory_space=pltpu.HBM)
    dma = lambda *d: pltpu.SemaphoreType.DMA(d)
    held = lambda a: pltpu.VMEM(a.shape, a.dtype)
    sketch, chosen, inverse = pl.pallas_call(
        functools.partial(sketch_kernel, rows, cols),
        out_shape=(
            pltpu.VMEM((width, leaf), F32),
            pltpu.VMEM((LEVELS + 1, width, k), F32),
            pltpu.VMEM((LEVELS, k, k), F32),
        ),
        in_specs=[hbm] * 8,
        out_specs=(vmem,) * 3,
        scratch_shapes=[
            held(sources), held(omega), held(leaf_pivots), held(p1), held(p2), held(p3),
            pltpu.VMEM((n, 2, targets.shape[1]), F32),
            pltpu.VMEM((cols, 1, leaf), jnp.int32),
            pltpu.VMEM((3, LANES, n * per), BF16),
            pltpu.VMEM((sources.shape[1], SIDE), BF16),
            pltpu.VMEM((width, leaf), F32),
            pltpu.VMEM((zs, width, leaf), F32),
            pltpu.VMEM((zs, width, leaf), F32),
            pltpu.VMEM((zs, width, leaf), BF16),
            pltpu.VMEM((zs, width, leaf), BF16),
            pltpu.VMEM((LEVELS, width, k), F32),
            pltpu.VMEM((LEVELS, width, k), F32),
            dma(8),
            dma(n), dma(n), dma(cols), dma(cols), dma(zs), dma(zs), dma(zs), dma(zs),
            dma(LEVELS), dma(LEVELS), dma(LEVELS), dma(LEVELS),
        ],
        compiler_params=pltpu.CompilerParams(
            collective_id=0, has_side_effects=True, vmem_limit_bytes=56 << 20
        ),
    )(targets, sources, omega, tree_order.reshape(1, leaf), leaf_pivots, p1, p2, p3)
    out_rows = [leaf] + [k // 2**s for s in range(LEVELS)]
    return pl.pallas_call(
        solve_kernel,
        out_shape=tuple(jax.ShapeDtypeStruct((r, k), F32) for r in out_rows)
        + (jax.ShapeDtypeStruct((k // 2**LEVELS, width), F32),),
        in_specs=[vmem] * 3,
        out_specs=(vmem,) * (len(out_rows) + 1),
        scratch_shapes=[
            pltpu.VMEM((k, k), F32),
            pltpu.VMEM((k, width), F32),
        ],
        compiler_params=pltpu.CompilerParams(vmem_limit_bytes=32 << 20),
    )(sketch, chosen, inverse)


def solution(mesh):
    both = P(("row", "col"), None)
    return jax.shard_map(
        functools.partial(body, mesh.shape["row"], mesh.shape["col"]),
        mesh=mesh,
        in_specs=(
            P(None, ("row", "col")),
            P(None, "col"),
            P(None, "col"),
            P(("row", "col")),
            both,
            P(),
            P(),
            P(),
        ),
        out_specs=(both,) * 5,
        check_vma=False,
    )
```

```python
import functools

import jax
import jax.numpy as jnp
from jax import lax
from jax.experimental import pallas as pl
from jax.experimental.pallas import tpu as pltpu
from jax.sharding import PartitionSpec as P

RIDGE = 0.1
DELTA_SQUARED = 0.0001
LEVELS = 3
LANES = 128
CHUNK = 512
SIDE = 16
LN2 = 0.6931471805599453
MESH = pl.DeviceIdType.MESH
HIGHEST = lax.Precision.HIGHEST
F32 = jnp.float32
BF16 = jnp.bfloat16


def split3(x):
    a = x.astype(BF16)
    r = x - a.astype(F32)
    b = r.astype(BF16)
    c = (r - b.astype(F32)).astype(BF16)
    return a, b, c


def pick(parts, hot):
    out = None
    for part in parts:
        term = jnp.dot(part, hot, preferred_element_type=F32)
        out = term if out is None else out + term
    return out


def flip(value, mask, bits):
    out = 0
    for i in range(bits):
        out = out + (value // 2**i + mask // 2**i) % 2 * 2**i
    return out


def sketch_kernel(
    rows, cols,
    tgt_hbm, src_hbm, om_hbm, ord_hbm, leaf_hbm, p1_hbm, p2_hbm, p3_hbm,
    rest_ref, ch_ref, inv_ref, place_ref,
    src_ref, om_ref, raw_ref, leaf_ref, p1_ref, p2_ref, p3_ref,
    every, orders, table, src_left, pts_a, pts_b,
    own_a, own_b, part_out_a, part_in_a, part_out_b, part_in_b,
    z_out_a, z_in_a, z_out_b, z_in_b, near_out, near_in, far_out, far_in,
    load_sem,
    tgt_send, tgt_recv, ord_send, ord_recv,
    pa_send, pa_recv, pb_send, pb_recv, za_send, za_recv, zb_send, zb_recv,
    ex_send, ex_recv,
):
    n = rows * cols
    zs = cols // 2
    bits = zs.bit_length() - 1
    row = lax.axis_index("row")
    col = lax.axis_index("col")
    me = row * cols + col
    z = col // 2
    core = col % 2
    partner = z * 2 + (1 - core)
    length = ord_hbm.shape[1]
    local = tgt_hbm.shape[1]
    k = leaf_hbm.shape[1]
    rest = length - k

    def load_of(i, src, dst):
        return pltpu.make_async_copy(src, dst, load_sem.at[i])

    early = [
        load_of(0, ord_hbm, raw_ref), load_of(1, leaf_hbm, leaf_ref),
        load_of(2, src_hbm, src_ref), load_of(3, tgt_hbm, every.at[me]),
    ]
    later = [
        load_of(4, om_hbm, om_ref), load_of(5, p1_hbm, p1_ref),
        load_of(6, p2_hbm, p2_ref), load_of(7, p3_hbm, p3_ref),
    ]
    for load in early + later:
        load.start()

    barrier = pltpu.get_barrier_semaphore()

    def greet(i, carry):
        other = lax.rem(me + i, n)
        pl.semaphore_signal(
            barrier, inc=1, device_id=(other // cols, other % cols), device_id_type=MESH
        )
        return carry

    lax.fori_loop(1, n, greet, 0)

    def pieces(x):
        return [p.astype(F32) for p in split3(x)]

    for load in early:
        load.wait()

    iota0 = lambda *d: lax.broadcasted_iota(jnp.int32, d, 0)
    iota1 = lambda *d: lax.broadcasted_iota(jnp.int32, d, 1)
    bf = lambda mask: mask.astype(F32).astype(BF16)

    is_pivot = (iota0(length, k) == leaf_ref[...]).astype(F32)
    taken = jnp.sum(is_pivot, axis=1, keepdims=True)
    at = jnp.sum(is_pivot * iota1(length, k).astype(F32), axis=1, keepdims=True)
    free = jnp.broadcast_to(1.0 - taken, (length, LANES)).astype(BF16)
    rank = jnp.dot(
        bf(iota1(length, length) < iota0(length, length)), free, preferred_element_type=F32
    )[:, 0:1]
    slot = jnp.where(taken > 0.5, at, rank + k)
    place = bf(slot == iota1(length, length).astype(F32))
    place_ref[...] = place
    raw = raw_ref[...]
    digits = jnp.concatenate(
        [raw % 128, raw // 128 % 128, raw // 16384] + [jnp.zeros_like(raw)] * 5, axis=0
    ).astype(F32).astype(BF16)
    moved = jnp.dot(digits, place, preferred_element_type=F32)
    orders[col] = (moved[0:1] + 128.0 * moved[1:2] + 16384.0 * moved[2:3]).astype(jnp.int32)

    wide = src_ref[...].astype(F32) - 0.5
    sx, sy = wide[0:1], wide[1:2]
    ones = jnp.ones_like(sx)
    left = []
    for part in (-2.0 * sx, -2.0 * sy):
        a, b, c = pieces(part)
        left += [a, a, b, b, c]
    left += pieces(sx * sx + sy * sy) + [ones] * 3
    src_left[...] = jnp.concatenate(left, axis=0).T.astype(BF16)

    pl.semaphore_wait(barrier, n - 1)

    def tgt_copy(i):
        other = lax.rem(me + i, n)
        return pltpu.make_async_remote_copy(
            src_ref=tgt_hbm, dst_ref=every.at[me],
            send_sem=tgt_send.at[i], recv_sem=tgt_recv.at[i],
            device_id=(other // cols, other % cols), device_id_type=MESH,
        )

    def ord_copy(i):
        other = lax.rem(col + i, cols)
        return pltpu.make_async_remote_copy(
            src_ref=orders.at[col], dst_ref=orders.at[col],
            send_sem=ord_send.at[i], recv_sem=ord_recv.at[i],
            device_id=(row, other), device_id_type=MESH,
        )

    def start(copy):
        def go(i, carry):
            copy(i).start()
            return carry
        return go

    def finish(copy):
        def go(i, carry):
            copy(i).wait()
            return carry
        return go

    lax.fori_loop(1, n, start(tgt_copy), 0)
    lax.fori_loop(1, cols, start(ord_copy), 0)
    for load in later:
        load.wait()
    lax.fori_loop(1, n, finish(tgt_copy), 0)
    lax.fori_loop(1, cols, finish(ord_copy), 0)

    spans = local // LANES
    for c in range(2):
        flat = jnp.concatenate(
            [every[:, c, a * LANES : (a + 1) * LANES] for a in range(spans)], axis=0
        ).T - 0.5
        high, low = halves(flat)
        table[c * LANES : (c + 1) * LANES, :] = jnp.concatenate([high, low], axis=1)

    for leaf in range(cols):
        order = orders[leaf]
        owner = order // LANES % spans * n + order // local
        lane = order % LANES
        hot = bf(iota0(n * spans, length) == owner)
        got = jnp.dot(
            table[...], jnp.concatenate([hot, hot], axis=0), preferred_element_type=F32
        )
        mine = iota0(LANES, length) == lane
        px, py = (
            jnp.sum(
                jnp.where(mine, got[c * LANES : (c + 1) * LANES], 0.0), axis=0, keepdims=True
            )
            for c in range(2)
        )
        right = []
        for part in (px, py):
            a, b = (h.astype(F32) for h in halves(part))
            right += [a, b, a, b, a]
        right += [jnp.ones_like(px)] * 3 + pieces(px * px + py * py + DELTA_SQUARED)
        points = jnp.concatenate(right, axis=0).astype(BF16)
        pts_a[leaf] = points[:, :k]
        pts_b[leaf] = points[:, k:]

    sources = src_ref.shape[1]

    def block(points, chunk):
        def squares(at):
            return jnp.dot(
                src_left[at : at + chunk, :], points, preferred_element_type=F32
            )

        total = None
        ahead = squares(0)
        for at in range(0, sources, chunk):
            now = ahead
            if at + chunk < sources:
                ahead = squares(at + chunk)
            panel = ((-0.5 * LN2) * jnp.log2(now)).astype(BF16)
            term = jnp.dot(
                om_ref[:, at : at + chunk], panel, preferred_element_type=F32
            )
            total = term if total is None else total + term
        return total

    class Stream:
        def __init__(self, pts, own, part_out, part_in, z_out, z_in, sems, size, chunk):
            self.__dict__.update(
                pts=pts, own=own, part_out=part_out, part_in=part_in, z_out=z_out,
                z_in=z_in, sems=sems, size=size, chunk=chunk,
            )

        def part_copy(self, x):
            return pltpu.make_async_remote_copy(
                src_ref=self.part_out.at[x], dst_ref=self.part_in.at[x],
                send_sem=self.sems[0].at[x], recv_sem=self.sems[1].at[x],
                device_id=(row, partner), device_id_type=MESH,
            )

        def z_copy(self, x, b):
            return pltpu.make_async_remote_copy(
                src_ref=self.z_out.at[x], dst_ref=self.z_in.at[x],
                send_sem=self.sems[2].at[x], recv_sem=self.sems[3].at[x],
                device_id=(row, flip(z, 2**b, bits) * 2 + core), device_id_type=MESH,
            )

        def compute(self, x):
            to = flip(z, x, bits)
            both = jnp.concatenate(
                [self.pts[to * 2 + core], self.pts[to * 2 + (1 - core)]], axis=1
            )
            total = block(both, self.chunk)
            self.part_out[x] = total[:, self.size :]
            self.part_copy(x).start()
            self.own[x] = total[:, : self.size]

        def total(self, x):
            low = bits if x == 0 else (x & -x).bit_length() - 1
            self.part_copy(x).wait()
            out = self.own[x] + self.part_in[x]
            for b in range(low):
                self.z_copy(x + 2**b, b).wait()
                out = out + self.z_in[x + 2**b].astype(F32)
            return out

        def pass_on(self, x):
            self.z_out[x] = self.total(x).astype(BF16)
            self.z_copy(x, (x & -x).bit_length() - 1).start()

    first = Stream(
        pts_a, own_a, part_out_a, part_in_a, z_out_a, z_in_a,
        (pa_send, pa_recv, za_send, za_recv), k, CHUNK // 2,
    )
    second = Stream(
        pts_b, own_b, part_out_b, part_in_b, z_out_b, z_in_b,
        (pb_send, pb_recv, zb_send, zb_recv), rest, CHUNK,
    )

    def ex_copy(s):
        bit = col // 2**s % 2
        out, into = (near_out, near_in) if s == 0 else (far_out.at[s - 1], far_in.at[s - 1])
        return pltpu.make_async_remote_copy(
            src_ref=out, dst_ref=into, send_sem=ex_send.at[s], recv_sem=ex_recv.at[s],
            device_id=(row, col + (1 - 2 * bit) * 2**s), device_id_type=MESH,
        )

    tables = (p1_ref, p2_ref, p3_ref)

    def offer(s, chosen):
        if s == 0:
            near_out[...] = chosen
        else:
            far_out[s - 1] = chosen.astype(BF16)
        ex_copy(s).start()

    def accept(s):
        bit = col // 2**s % 2
        pivots = tables[s][pl.ds(me // 2 ** (s + 1), 1), :]
        index = iota0(k, k)
        own = pick(split3(ch_ref[s]), bf(index + bit * k == pivots))
        hot = bf(index + (1 - bit) * k == pivots)
        ex_copy(s).wait()
        theirs = split3(near_in[...]) if s == 0 else [far_in[s - 1]]
        chosen = own + pick(theirs, hot)
        ch_ref[s + 1] = chosen
        return chosen

    seq = []
    for b in range(bits):
        count = zs // 2 ** (b + 1)
        seq += [(2 * (count - 1 - j) + 1) * 2**b for j in range(count)]
    seq.append(0)

    for i, x in enumerate(seq):
        first.compute(x)
        if i > 0 and seq[i - 1] % 2 == 1:
            first.pass_on(seq[i - 1])
    done = 0
    for x in seq:
        if x > 0 and x % 2 == 0:
            second.compute(seq[done])
            done += 1
            first.pass_on(x)
    sent = 0
    while done < zs - 1:
        second.compute(seq[done])
        done += 1
        if sent < 1:
            second.pass_on(seq[sent])
            sent += 1
    chosen = first.total(0)
    ch_ref[0] = chosen
    offer(0, chosen)
    second.compute(0)
    offer(1, accept(0))
    while seq[sent] % 2 == 1:
        second.pass_on(seq[sent])
        sent += 1
    offer(2, accept(1))
    while seq[sent] > 0:
        second.pass_on(seq[sent])
        sent += 1
    inverse = shifted_inverses([contract0(ch_ref[m], ch_ref[m]) for m in range(LEVELS)])
    for m in range(LEVELS):
        inv_ref[m] = inverse[m]
    top = accept(2)
    inv_ref[LEVELS] = shifted_inverses([contract0(top, top)])[0]
    rest_ref[...] = second.total(0)


def contract0(a, b):
    return lax.dot_general(
        a, b, (((0,), (0,)), ((), ())), precision=HIGHEST, preferred_element_type=F32
    )


def halves(x):
    h = x.astype(BF16)
    return h, (x - h.astype(F32)).astype(BF16)


def product3(a, b):
    ah, al = halves(a)
    bh, bl = halves(b)
    dot = functools.partial(jnp.dot, preferred_element_type=F32)
    return dot(ah, bh) + (dot(ah, bl) + dot(al, bh))


def product6(a, b):
    return jnp.dot(a, b, precision=HIGHEST, preferred_element_type=F32)


def shifted_inverses(grams):
    k = grams[0].shape[0]
    eye = lax.broadcasted_iota(jnp.int32, (k, k), 0) == lax.broadcasted_iota(
        jnp.int32, (k, k), 1
    )
    one = jnp.where(eye, 1.0, 0.0)
    low = 1.0 / (k / RIDGE + 1.0)
    gap = (1.0 - low) / (1.0 + low)
    first = 2.0 / (1.0 + low)
    tops, mats = [], []
    for gram in grams:
        trace = jnp.sum(jnp.where(eye, gram, 0.0), axis=(0, 1), keepdims=True)
        shift = RIDGE * (trace / k + 1e-06)
        tops.append(trace + shift)
        mats.append((gram + shift * one) / (trace + shift))
    scale = 2.0 / (2.0 - gap * gap)
    xs = [scale * (2.0 * first * one - first * first * m) for m in mats]
    gap = gap * gap / (2.0 - gap * gap)
    scales = []
    while gap > 1e-9:
        scales.append(2.0 / (2.0 - gap * gap))
        gap = gap * gap / (2.0 - gap * gap)
    for i, scale in enumerate(scales):
        product = product6 if i >= len(scales) - 2 else product3
        ys = [scale * (2.0 * one - product(m, x)) for m, x in zip(mats, xs)]
        xs = [product(x, y) for x, y in zip(xs, ys)]
    return [x / t for x, t in zip(xs, tops)]


def solve_kernel(rest_ref, ch_ref, inv_ref, place_ref, o0, o1, o2, o3, root, r_ref, t_ref):
    col = lax.axis_index("col")
    levels = ch_ref.shape[0]
    ahead = jnp.concatenate(
        [contract0(ch_ref[0], ch_ref[0]), contract0(rest_ref[...], ch_ref[0])], axis=0
    )
    sorted_rows = product6(ahead, inv_ref[0])
    o0[...] = sum(
        jnp.dot(place_ref[...], part, preferred_element_type=F32)
        for part in split3(sorted_rows)
    )
    for s, o in enumerate((o1, o2, o3)):
        r_ref[...] = contract0(ch_ref[s], ch_ref[s + 1])
        size = o.shape[0]
        at = pl.multiple_of(col % 2**s * size, size)
        o[...] = product6(r_ref[pl.ds(at, size), :], inv_ref[s + 1])
    t_ref[...] = ch_ref[levels - 1].T
    size = root.shape[0]
    root[...] = t_ref[pl.ds(pl.multiple_of(col % 2**LEVELS * size, size), size), :]


def body(rows, cols, targets, sources, omega, tree_order, leaf_pivots, p1, p2, p3):
    n = rows * cols
    zs = cols // 2
    leaf = tree_order.shape[0]
    width = omega.shape[0]
    k = leaf_pivots.shape[1]
    rest = leaf - k
    spans = targets.shape[1] // LANES
    vmem = pl.BlockSpec(memory_space=pltpu.VMEM)
    hbm = pl.BlockSpec(memory_space=pltpu.HBM)
    dma = lambda *d: pltpu.SemaphoreType.DMA(d)
    held = lambda a: pltpu.VMEM(a.shape, a.dtype)
    order = tree_order.reshape(1, leaf)
    kept = pl.pallas_call(
        functools.partial(sketch_kernel, rows, cols),
        out_shape=(
            pltpu.VMEM((width, rest), F32),
            pltpu.VMEM((LEVELS + 1, width, k), F32),
            pltpu.VMEM((LEVELS + 1, k, k), F32),
            pltpu.VMEM((leaf, leaf), BF16),
        ),
        in_specs=[hbm] * 8,
        out_specs=(vmem,) * 4,
        scratch_shapes=[
            held(sources), held(omega), held(order), held(leaf_pivots),
            held(p1), held(p2), held(p3),
            pltpu.VMEM((n, 2, targets.shape[1]), F32),
            pltpu.VMEM((cols, 1, leaf), jnp.int32),
            pltpu.VMEM((2 * LANES, 2 * n * spans), BF16),
            pltpu.VMEM((sources.shape[1], SIDE), BF16),
            pltpu.VMEM((cols, SIDE, k), BF16),
            pltpu.VMEM((cols, SIDE, rest), BF16),
            pltpu.VMEM((zs, width, k), F32),
            pltpu.VMEM((zs, width, rest), F32),
            pltpu.VMEM((zs, width, k), F32),
            pltpu.VMEM((zs, width, k), F32),
            pltpu.VMEM((zs, width, rest), F32),
            pltpu.VMEM((zs, width, rest), F32),
            pltpu.VMEM((zs, width, k), BF16),
            pltpu.VMEM((zs, width, k), BF16),
            pltpu.VMEM((zs, width, rest), BF16),
            pltpu.VMEM((zs, width, rest), BF16),
            pltpu.VMEM((width, k), F32),
            pltpu.VMEM((width, k), F32),
            pltpu.VMEM((LEVELS - 1, width, k), BF16),
            pltpu.VMEM((LEVELS - 1, width, k), BF16),
            dma(8),
            dma(n), dma(n), dma(cols), dma(cols),
            dma(zs), dma(zs), dma(zs), dma(zs), dma(zs), dma(zs), dma(zs), dma(zs),
            dma(LEVELS), dma(LEVELS),
        ],
        compiler_params=pltpu.CompilerParams(
            collective_id=0, has_side_effects=True, vmem_limit_bytes=60 << 20
        ),
    )(targets, sources, omega, order, leaf_pivots, p1, p2, p3)
    out_rows = [leaf] + [k // 2**s for s in range(LEVELS)]
    return pl.pallas_call(
        solve_kernel,
        out_shape=tuple(jax.ShapeDtypeStruct((r, k), F32) for r in out_rows)
        + (jax.ShapeDtypeStruct((k // 2**LEVELS, width), F32),),
        in_specs=[vmem] * 4,
        out_specs=(vmem,) * (len(out_rows) + 1),
        scratch_shapes=[
            pltpu.VMEM((k, k), F32),
            pltpu.VMEM((k, width), F32),
        ],
        compiler_params=pltpu.CompilerParams(vmem_limit_bytes=32 << 20),
    )(*kept)


def solution(mesh):
    both = P(("row", "col"), None)
    return jax.shard_map(
        functools.partial(body, mesh.shape["row"], mesh.shape["col"]),
        mesh=mesh,
        in_specs=(
            P(None, ("row", "col")),
            P(None, "col"),
            P(None, "col"),
            P(("row", "col")),
            both,
            P(),
            P(),
            P(),
        ),
        out_specs=(both,) * 5,
        check_vma=False,
    )
```

```python
import functools

import jax
import jax.numpy as jnp
from jax import lax
from jax.experimental import pallas as pl
from jax.experimental.pallas import tpu as pltpu
from jax.sharding import PartitionSpec as P

RIDGE = 0.1
DELTA_SQUARED = 0.0001
LEVELS = 3
LANES = 128
CHUNK = 512
SIDE = 16
STREAM_REFS = 9
PLAN = (
    "A3 C3 pA3 A1 A2 pC3 A0 pA2 pA1 C2 B3 B2 pC2 pB3 B1",
    "o0 C1 a0 B0 pB2 C0 a1 pB1 pC1",
)
LN2 = 0.6931471805599453
MESH = pl.DeviceIdType.MESH
HIGHEST = lax.Precision.HIGHEST
F32 = jnp.float32
BF16 = jnp.bfloat16


def split3(x):
    a = x.astype(BF16)
    r = x - a.astype(F32)
    b = r.astype(BF16)
    c = (r - b.astype(F32)).astype(BF16)
    return a, b, c


def pick(parts, hot):
    out = None
    for part in parts:
        term = jnp.dot(part, hot, preferred_element_type=F32)
        out = term if out is None else out + term
    return out


def flip(value, mask, bits):
    out = 0
    for i in range(bits):
        out = out + (value // 2**i + mask // 2**i) % 2 * 2**i
    return out


def sketch_kernel(
    rows, cols,
    tgt_hbm, src_hbm, om_hbm, ord_hbm, leaf_hbm, p1_hbm, p2_hbm, p3_hbm,
    rest_ref, g_ref, base_ref, place_ref, o1_ref, o2_ref, o3_ref, root_ref,
    src_ref, om_ref, raw_ref, leaf_ref, p1_ref, p2_ref, p3_ref,
    every, orders, table, src_left, ch_ref, r_ref, t_ref,
    *scratch,
):
    streamed, scratch = scratch[: 3 * STREAM_REFS], scratch[3 * STREAM_REFS :]
    (
        near_out, near_in, far_out, far_in, load_sem, tgt_send, tgt_recv, ord_send, ord_recv,
        ex_send, ex_recv,
    ) = scratch
    n = rows * cols
    zs = cols // 2
    bits = zs.bit_length() - 1
    row = lax.axis_index("row")
    col = lax.axis_index("col")
    me = row * cols + col
    z = col // 2
    core = col % 2
    partner = z * 2 + (1 - core)
    length = ord_hbm.shape[1]
    local = tgt_hbm.shape[1]
    k = leaf_hbm.shape[1]
    rest = length - k

    def load_of(i, src, dst):
        return pltpu.make_async_copy(src, dst, load_sem.at[i])

    early = [
        load_of(0, ord_hbm, raw_ref), load_of(1, leaf_hbm, leaf_ref),
        load_of(2, src_hbm, src_ref), load_of(3, tgt_hbm, every.at[me]),
    ]
    later = [
        load_of(4, om_hbm, om_ref), load_of(5, p1_hbm, p1_ref),
        load_of(6, p2_hbm, p2_ref), load_of(7, p3_hbm, p3_ref),
    ]
    for load in early + later:
        load.start()

    barrier = pltpu.get_barrier_semaphore()

    def away(mask):
        out_row, out_col = row, col
        for b in range((cols - 1).bit_length()):
            if mask >> b & 1:
                out_col = out_col + (1 - 2 * (col // 2**b % 2)) * 2**b
        for b in range((rows - 1).bit_length()):
            if mask // cols >> b & 1:
                out_row = out_row + (1 - 2 * (row // 2**b % 2)) * 2**b
        return out_row, out_col

    def for_others(go):
        if n <= 64:
            for mask in range(n - 1, 0, -1):
                go(away(mask))
        else:

            def step(i, carry):
                other = lax.rem(me + i, n)
                go((other // cols, other % cols))
                return carry

            lax.fori_loop(1, n, step, 0)

    def greet(device):
        pl.semaphore_signal(barrier, inc=1, device_id=device, device_id_type=MESH)

    for_others(greet)

    def pieces(x):
        return [p.astype(F32) for p in split3(x)]

    for load in early:
        load.wait()

    iota0 = lambda *d: lax.broadcasted_iota(jnp.int32, d, 0)
    iota1 = lambda *d: lax.broadcasted_iota(jnp.int32, d, 1)
    bf = lambda mask: mask.astype(F32).astype(BF16)

    is_pivot = (iota0(length, k) == leaf_ref[...]).astype(F32)
    taken = jnp.sum(is_pivot, axis=1, keepdims=True)
    at = jnp.sum(is_pivot * iota1(length, k).astype(F32), axis=1, keepdims=True)
    free = jnp.broadcast_to(1.0 - taken, (length, LANES)).astype(BF16)
    rank = jnp.dot(
        bf(iota1(length, length) < iota0(length, length)), free, preferred_element_type=F32
    )[:, 0:1]
    slot = jnp.where(taken > 0.5, at, rank + k)
    place = bf(slot == iota1(length, length).astype(F32))
    place_ref[...] = place[:, k:]
    base_place = place[:, :k]
    raw = raw_ref[...]
    digits = jnp.concatenate(
        [raw % 128, raw // 128 % 128, raw // 16384] + [jnp.zeros_like(raw)] * 5, axis=0
    ).astype(F32).astype(BF16)
    moved = jnp.dot(digits, place, preferred_element_type=F32)
    orders[col] = (moved[0:1] + 128.0 * moved[1:2] + 16384.0 * moved[2:3]).astype(jnp.int32)

    wide = src_ref[...].astype(F32) - 0.5
    sx, sy = wide[0:1], wide[1:2]
    ones = jnp.ones_like(sx)
    left = []
    for part in (-2.0 * sx, -2.0 * sy):
        a, b, c = pieces(part)
        left += [a, a, b, b, c]
    left += pieces(sx * sx + sy * sy) + [ones] * 3
    src_left[...] = jnp.concatenate(left, axis=0).T.astype(BF16)

    pl.semaphore_wait(barrier, n - 1)

    def tgt_copy(device, src, dst):
        return pltpu.make_async_remote_copy(
            src_ref=src, dst_ref=dst, send_sem=tgt_send, recv_sem=tgt_recv,
            device_id=device, device_id_type=MESH,
        )

    def ord_copy(device, src, dst):
        return pltpu.make_async_remote_copy(
            src_ref=src, dst_ref=dst, send_sem=ord_send, recv_sem=ord_recv,
            device_id=device, device_id_type=MESH,
        )

    for_others(lambda device: tgt_copy(device, tgt_hbm, every.at[me]).start())
    for mask in range(cols - 1, 0, -1):
        ord_copy(away(mask), orders.at[col], orders.at[col]).start()
    for load in later:
        load.wait()
    whole = every.at[pl.ds(0, n - 1)]
    tgt_copy((row, partner), whole, whole).wait()
    whole = orders.at[pl.ds(0, cols - 1)]
    ord_copy((row, partner), whole, whole).wait()

    spans = local // LANES
    for c in range(2):
        flat = jnp.concatenate(
            [every[:, c, a * LANES : (a + 1) * LANES] for a in range(spans)], axis=0
        ).T - 0.5
        high, low = halves(flat)
        table[c * LANES : (c + 1) * LANES, :] = jnp.concatenate([high, low], axis=1)

    def points_of(order):
        length = order.shape[1]
        owner = order // LANES % spans * n + order // local
        lane = order % LANES
        hot = bf(iota0(n * spans, length) == owner)
        got = jnp.dot(
            table[...], jnp.concatenate([hot, hot], axis=0), preferred_element_type=F32
        )
        mine = iota0(LANES, length) == lane
        px, py = (
            jnp.sum(
                jnp.where(mine, got[c * LANES : (c + 1) * LANES], 0.0), axis=0, keepdims=True
            )
            for c in range(2)
        )
        right = []
        for part in (px, py):
            a, b = (h.astype(F32) for h in halves(part))
            right += [a, b, a, b, a]
        right += [jnp.ones_like(px)] * 3 + pieces(px * px + py * py + DELTA_SQUARED)
        return jnp.concatenate(right, axis=0).astype(BF16)

    sources = src_ref.shape[1]

    def block(order, chunk):
        points = points_of(order)

        def squares(at):
            return jnp.dot(
                src_left[at : at + chunk, :], points, preferred_element_type=F32
            )

        total = None
        ahead = squares(0)
        for at in range(0, sources, chunk):
            now = ahead
            if at + chunk < sources:
                ahead = squares(at + chunk)
            panel = ((-0.5 * LN2) * jnp.log2(now)).astype(BF16)
            term = jnp.dot(
                om_ref[:, at : at + chunk], panel, preferred_element_type=F32
            )
            total = term if total is None else total + term
        return total

    class Stream:
        def __init__(self, start, refs):
            self.start = start
            self.own, self.part_out, self.part_in, self.z_out, self.z_in = refs[:5]
            self.sems = refs[5:]

        def compute(self, x):
            to = flip(z, x, bits)
            size = self.own.shape[2]
            mine, theirs = (
                orders[leaf][:, self.start : self.start + size]
                for leaf in (to * 2 + core, to * 2 + (1 - core))
            )
            total = block(
                jnp.concatenate([theirs, mine], axis=1), min(CHUNK, 2 * size)
            )
            self.part_out[x] = total[:, :size]
            self.part_copy(x).start()
            self.own[x] = total[:, size:]

        def part_copy(self, x):
            return pltpu.make_async_remote_copy(
                src_ref=self.part_out.at[x], dst_ref=self.part_in.at[x],
                send_sem=self.sems[0].at[x], recv_sem=self.sems[1].at[x],
                device_id=(row, partner), device_id_type=MESH,
            )

        def z_copy(self, x, b):
            return pltpu.make_async_remote_copy(
                src_ref=self.z_out.at[x], dst_ref=self.z_in.at[x],
                send_sem=self.sems[2].at[x], recv_sem=self.sems[3].at[x],
                device_id=(row, flip(z, 2**b, bits) * 2 + core), device_id_type=MESH,
            )

        def total(self, x):
            low = bits if x == 0 else (x & -x).bit_length() - 1
            self.part_copy(x).wait()
            out = self.own[x] + self.part_in[x]
            for b in range(low):
                self.z_copy(x + 2**b, b).wait()
                out = out + self.z_in[x + 2**b].astype(F32)
            return out

        def pass_on(self, x):
            self.z_out[x] = self.total(x).astype(BF16)
            self.z_copy(x, (x & -x).bit_length() - 1).start()

    starts = (0, k, k + streamed[STREAM_REFS].shape[2])
    streams = {
        name: Stream(at, streamed[i * STREAM_REFS : (i + 1) * STREAM_REFS])
        for i, (name, at) in enumerate(zip("ABC", starts))
    }

    def ex_copy(s):
        bit = col // 2**s % 2
        out, into = (near_out, near_in) if s == 0 else (far_out.at[s - 1], far_in.at[s - 1])
        return pltpu.make_async_remote_copy(
            src_ref=out, dst_ref=into, send_sem=ex_send.at[s], recv_sem=ex_recv.at[s],
            device_id=(row, col + (1 - 2 * bit) * 2**s), device_id_type=MESH,
        )

    tables = (p1_ref, p2_ref, p3_ref)

    def offer(s, chosen):
        if s == 0:
            near_out[...] = chosen
        else:
            far_out[s - 1] = chosen.astype(BF16)
        ex_copy(s).start()

    def accept(s):
        bit = col // 2**s % 2
        pivots = tables[s][pl.ds(me // 2 ** (s + 1), 1), :]
        index = iota0(k, k)
        own = pick(split3(ch_ref[s]), bf(index + bit * k == pivots))
        hot = bf(index + (1 - bit) * k == pivots)
        ex_copy(s).wait()
        theirs = split3(near_in[...]) if s == 0 else [far_in[s - 1]]
        chosen = own + pick(theirs, hot)
        ch_ref[s + 1] = chosen
        return chosen

    seq = []
    for b in range(bits):
        count = zs // 2 ** (b + 1)
        seq += [(2 * (count - 1 - j) + 1) * 2**b for j in range(count)]
    seq.append(0)

    if zs == 4:
        plan = " ".join(PLAN).split()
    else:
        plan = []
        for name in "ABC":
            for i, x in enumerate(seq):
                plan += [f"{name}{x}"] + [f"p{name}{y}" for y in seq[i - 1 : i]]
        plan += ["o0", "a0", "a1"]
    for step in plan:
        kind, index = step[:-1], int(step[-1])
        if kind in streams:
            streams[kind].compute(index)
        elif kind[0] == "p":
            streams[kind[1]].pass_on(index)
        elif kind == "o":
            ch_ref[0] = streams["A"].total(0)
            offer(0, ch_ref[0])
        else:
            offer(index + 1, accept(index))
    grams = [contract0(ch_ref[m], ch_ref[m]) for m in range(LEVELS)]
    inverse = shifted_inverses(grams)
    g_ref[...] = product6(ch_ref[0], inverse[0])
    base_ref[...] = placed(base_place, product6(grams[0], inverse[0]))

    def interpolate(s, o_ref, inv):
        r_ref[...] = contract0(ch_ref[s], ch_ref[s + 1])
        size = o_ref.shape[0]
        at = pl.multiple_of(col % 2**s * size, size)
        o_ref[...] = product6(r_ref[pl.ds(at, size), :], inv)

    interpolate(0, o1_ref, inverse[1])
    interpolate(1, o2_ref, inverse[2])
    top = accept(2)
    t_ref[...] = top.T
    size = root_ref.shape[0]
    root_ref[...] = t_ref[pl.ds(pl.multiple_of(col % 2**LEVELS * size, size), size), :]
    interpolate(2, o3_ref, shifted_inverses([contract0(top, top)])[0])
    edge = starts[2] - k
    rest_ref[:, :edge] = streams["B"].total(0)
    rest_ref[:, edge:] = streams["C"].total(0)


def placed(place, x):
    high, low = halves(x)
    both = jnp.dot(
        place, jnp.concatenate([high, low], axis=1), preferred_element_type=F32
    )
    return both[:, : x.shape[1]] + both[:, x.shape[1] :]


def contract0(a, b):
    return lax.dot_general(
        a, b, (((0,), (0,)), ((), ())), precision=HIGHEST, preferred_element_type=F32
    )


def halves(x):
    h = x.astype(BF16)
    return h, (x - h.astype(F32)).astype(BF16)


def product4(a, b):
    k = b.shape[1]
    right = jnp.concatenate(halves(b), axis=1)
    both = jnp.dot(
        jnp.concatenate(halves(a), axis=1),
        jnp.concatenate([right, right], axis=0),
        preferred_element_type=F32,
    )
    return both[:, :k] + both[:, k:]


def product6(a, b):
    return jnp.dot(a, b, precision=HIGHEST, preferred_element_type=F32)


def shifted_inverses(grams):
    k = grams[0].shape[0]
    eye = lax.broadcasted_iota(jnp.int32, (k, k), 0) == lax.broadcasted_iota(
        jnp.int32, (k, k), 1
    )
    one = jnp.where(eye, 1.0, 0.0)
    low = 1.0 / (k / RIDGE + 1.0)
    gap = (1.0 - low) / (1.0 + low)
    first = 2.0 / (1.0 + low)
    tops, mats = [], []
    for gram in grams:
        trace = jnp.sum(jnp.where(eye, gram, 0.0), axis=(0, 1), keepdims=True)
        shift = RIDGE * (trace / k + 1e-06)
        tops.append(trace + shift)
        mats.append((gram + shift * one) / (trace + shift))
    scale = 2.0 / (2.0 - gap * gap)
    xs = [scale * (2.0 * first * one - first * first * m) for m in mats]
    gap = gap * gap / (2.0 - gap * gap)
    scales = []
    while gap > 2e-6:
        scales.append(2.0 / (2.0 - gap * gap))
        gap = gap * gap / (2.0 - gap * gap)
    pairs = [jnp.concatenate([product4(m, x), x], axis=0) for m, x in zip(mats, xs)]
    for scale in scales[:-2]:
        ys = [scale * (2.0 * one - pair[:k]) for pair in pairs]
        pairs = [product4(pair, y) for pair, y in zip(pairs, ys)]
    xs = [pair[k:] for pair in pairs]
    for scale in scales[-2:]:
        ys = [scale * (2.0 * one - product6(m, x)) for m, x in zip(mats, xs)]
        xs = [product4(x, y) for x, y in zip(xs, ys)]
    return [x / t for x, t in zip(xs, tops)]


def solve_kernel(
    rest_ref, g_ref, base_ref, place_ref, i1, i2, i3, top, o0, o1, o2, o3, root
):
    for got, o in ((i1, o1), (i2, o2), (i3, o3), (top, root)):
        o[...] = got[...]
    o0[...] = base_ref[...] + placed(place_ref[...], contract0(rest_ref[...], g_ref[...]))


def body(rows, cols, targets, sources, omega, tree_order, leaf_pivots, p1, p2, p3):
    n = rows * cols
    zs = cols // 2
    leaf = tree_order.shape[0]
    width = omega.shape[0]
    k = leaf_pivots.shape[1]
    rest = leaf - k
    spans = targets.shape[1] // LANES
    vmem = pl.BlockSpec(memory_space=pltpu.VMEM)
    hbm = pl.BlockSpec(memory_space=pltpu.HBM)
    dma = lambda *d: pltpu.SemaphoreType.DMA(d)
    held = lambda a: pltpu.VMEM(a.shape, a.dtype)
    order = tree_order.reshape(1, leaf)

    def stream(size):
        wide, narrow = (pltpu.VMEM((zs, width, size), t) for t in (F32, BF16))
        return [wide, wide, wide, narrow, narrow] + [dma(zs)] * 4

    out_rows = [leaf] + [k // 2**s for s in range(LEVELS)]
    kept = pl.pallas_call(
        functools.partial(sketch_kernel, rows, cols),
        out_shape=(
            pltpu.VMEM((width, rest), F32),
            pltpu.VMEM((width, k), F32),
            pltpu.VMEM((leaf, k), F32),
            pltpu.VMEM((leaf, rest), BF16),
        )
        + tuple(pltpu.VMEM((r, k), F32) for r in out_rows[1:])
        + (pltpu.VMEM((k // 2**LEVELS, width), F32),),
        in_specs=[hbm] * 8,
        out_specs=(vmem,) * (LEVELS + 5),
        scratch_shapes=[
            held(sources), held(omega), held(order), held(leaf_pivots),
            held(p1), held(p2), held(p3),
            pltpu.VMEM((n, 2, targets.shape[1]), F32),
            pltpu.VMEM((cols, 1, leaf), jnp.int32),
            pltpu.VMEM((2 * LANES, 2 * n * spans), BF16),
            pltpu.VMEM((sources.shape[1], SIDE), BF16),
            pltpu.VMEM((LEVELS + 1, width, k), F32),
            pltpu.VMEM((k, k), F32),
            pltpu.VMEM((k, width), F32),
            *stream(k), *stream(LANES), *stream(rest - LANES),
            pltpu.VMEM((width, k), F32),
            pltpu.VMEM((width, k), F32),
            pltpu.VMEM((LEVELS - 1, width, k), BF16),
            pltpu.VMEM((LEVELS - 1, width, k), BF16),
            dma(8),
            pltpu.SemaphoreType.DMA, pltpu.SemaphoreType.DMA,
            pltpu.SemaphoreType.DMA, pltpu.SemaphoreType.DMA,
            dma(LEVELS), dma(LEVELS),
        ],
        compiler_params=pltpu.CompilerParams(
            collective_id=0, has_side_effects=True, vmem_limit_bytes=60 << 20
        ),
    )(targets, sources, omega, order, leaf_pivots, p1, p2, p3)
    return pl.pallas_call(
        solve_kernel,
        out_shape=tuple(jax.ShapeDtypeStruct((r, k), F32) for r in out_rows)
        + (jax.ShapeDtypeStruct((k // 2**LEVELS, width), F32),),
        in_specs=[vmem] * len(kept),
        out_specs=(vmem,) * (len(out_rows) + 1),
        compiler_params=pltpu.CompilerParams(vmem_limit_bytes=32 << 20),
    )(*kept)


def solution(mesh):
    both = P(("row", "col"), None)
    return jax.shard_map(
        functools.partial(body, mesh.shape["row"], mesh.shape["col"]),
        mesh=mesh,
        in_specs=(
            P(None, ("row", "col")),
            P(None, "col"),
            P(None, "col"),
            P(("row", "col")),
            both,
            P(),
            P(),
            P(),
        ),
        out_specs=(both,) * 5,
        check_vma=False,
    )
```

```python
import functools

import jax
import jax.numpy as jnp
from jax import lax
from jax.experimental import pallas as pl
from jax.experimental.pallas import tpu as pltpu
from jax.sharding import PartitionSpec as P

RIDGE = 0.1
DELTA_SQUARED = 0.0001
LEVELS = 3
LANES = 128
CHUNK = 512
SIDE = 16
STREAM_REFS = 9
PLAN = (
    "A3B3 C3 pA3 A1B1 pC3 A2B2 pA1 C2 pA2 A0B0 pC2 pB3 C1",
    "o0 C0 a0 pB1 i0 r0 pC1 pB2 a1",
)
GROUP = 2 ** (LEVELS - 1)
LN2 = 0.6931471805599453
MESH = pl.DeviceIdType.MESH
HIGHEST = lax.Precision.HIGHEST
F32 = jnp.float32
BF16 = jnp.bfloat16


def split3(x):
    a = x.astype(BF16)
    r = x - a.astype(F32)
    b = r.astype(BF16)
    c = (r - b.astype(F32)).astype(BF16)
    return a, b, c


def pick(parts, hot):
    out = None
    for part in parts:
        term = jnp.dot(part, hot, preferred_element_type=F32)
        out = term if out is None else out + term
    return out


def flip(value, mask, bits):
    out = 0
    for i in range(bits):
        out = out + (value // 2**i + mask // 2**i) % 2 * 2**i
    return out


def sketch_kernel(
    rows, cols,
    tgt_hbm, src_hbm, om_hbm, ord_hbm, leaf_hbm, p1_hbm, p2_hbm, p3_hbm,
    rest_ref, g_ref, base_ref, place_ref, o1_ref, o2_ref, o3_ref, root_ref,
    src_ref, om_ref, raw_ref, leaf_ref, p1_ref, p2_ref, p3_ref,
    every, orders, table, src_left, ch_ref, r_ref, t_ref,
    *scratch,
):
    streamed, scratch = scratch[: 3 * STREAM_REFS], scratch[3 * STREAM_REFS :]
    (
        near_out, near_in, far_out, far_in, load_sem, tgt_send, tgt_recv, ord_send, ord_recv,
        near_send, near_recv, far_send, far_recv, pass_send, pass_recv,
    ) = scratch
    n = rows * cols
    zs = cols // 2
    bits = zs.bit_length() - 1
    row = lax.axis_index("row")
    col = lax.axis_index("col")
    me = row * cols + col
    z = col // 2
    core = col % 2
    partner = z * 2 + (1 - core)
    length = ord_hbm.shape[1]
    local = tgt_hbm.shape[1]
    k = leaf_hbm.shape[1]
    rest = length - k

    def load_of(i, src, dst):
        return pltpu.make_async_copy(src, dst, load_sem.at[i])

    early = [
        load_of(0, ord_hbm, raw_ref), load_of(1, leaf_hbm, leaf_ref),
        load_of(2, src_hbm, src_ref), load_of(3, tgt_hbm, every.at[me]),
    ]
    later = [
        load_of(4, om_hbm, om_ref), load_of(5, p1_hbm, p1_ref),
        load_of(6, p2_hbm, p2_ref), load_of(7, p3_hbm, p3_ref),
    ]
    for load in early + later:
        load.start()

    barrier = pltpu.get_barrier_semaphore()

    def away(mask):
        out_row, out_col = row, col
        for b in range((cols - 1).bit_length()):
            if mask >> b & 1:
                out_col = out_col + (1 - 2 * (col // 2**b % 2)) * 2**b
        for b in range((rows - 1).bit_length()):
            if mask // cols >> b & 1:
                out_row = out_row + (1 - 2 * (row // 2**b % 2)) * 2**b
        return out_row, out_col

    def for_others(go):
        if n <= 64:
            for mask in range(n - 1, 0, -1):
                go(away(mask))
        else:

            def step(i, carry):
                other = lax.rem(me + i, n)
                go((other // cols, other % cols))
                return carry

            lax.fori_loop(1, n, step, 0)

    def greet(device):
        pl.semaphore_signal(barrier, inc=1, device_id=device, device_id_type=MESH)

    for_others(greet)

    def pieces(x):
        return [p.astype(F32) for p in split3(x)]

    for load in early:
        load.wait()

    iota0 = lambda *d: lax.broadcasted_iota(jnp.int32, d, 0)
    iota1 = lambda *d: lax.broadcasted_iota(jnp.int32, d, 1)
    bf = lambda mask: mask.astype(F32).astype(BF16)

    is_pivot = (iota0(length, k) == leaf_ref[...]).astype(F32)
    taken = jnp.sum(is_pivot, axis=1, keepdims=True)
    at = jnp.sum(is_pivot * iota1(length, k).astype(F32), axis=1, keepdims=True)
    free = jnp.broadcast_to(1.0 - taken, (length, LANES)).astype(BF16)
    rank = jnp.dot(
        bf(iota1(length, length) < iota0(length, length)), free, preferred_element_type=F32
    )[:, 0:1]
    slot = jnp.where(taken > 0.5, at, rank + k)
    place = bf(slot == iota1(length, length).astype(F32))
    place_ref[...] = place[:, k:]
    base_place = place[:, :k]
    raw = raw_ref[...]
    digits = jnp.concatenate(
        [raw % 128, raw // 128 % 128, raw // 16384] + [jnp.zeros_like(raw)] * 5, axis=0
    ).astype(F32).astype(BF16)
    moved = jnp.dot(digits, place, preferred_element_type=F32)
    orders[col] = (moved[0:1] + 128.0 * moved[1:2] + 16384.0 * moved[2:3]).astype(jnp.int32)

    wide = src_ref[...].astype(F32) - 0.5
    sx, sy = wide[0:1], wide[1:2]
    ones = jnp.ones_like(sx)
    left = []
    for part in (-2.0 * sx, -2.0 * sy):
        a, b, c = pieces(part)
        left += [a, a, b, b, c]
    left += pieces(sx * sx + sy * sy) + [ones] * 3
    src_left[...] = jnp.concatenate(left, axis=0).T.astype(BF16)

    pl.semaphore_wait(barrier, n - 1)

    def tgt_copy(device, src, dst):
        return pltpu.make_async_remote_copy(
            src_ref=src, dst_ref=dst, send_sem=tgt_send, recv_sem=tgt_recv,
            device_id=device, device_id_type=MESH,
        )

    def ord_copy(device, src, dst):
        return pltpu.make_async_remote_copy(
            src_ref=src, dst_ref=dst, send_sem=ord_send, recv_sem=ord_recv,
            device_id=device, device_id_type=MESH,
        )

    for_others(lambda device: tgt_copy(device, tgt_hbm, every.at[me]).start())
    for mask in range(cols - 1, 0, -1):
        ord_copy(away(mask), orders.at[col], orders.at[col]).start()
    for load in later:
        load.wait()
    whole = every.at[pl.ds(0, n - 1)]
    tgt_copy((row, partner), whole, whole).wait()
    whole = orders.at[pl.ds(0, cols - 1)]
    ord_copy((row, partner), whole, whole).wait()

    spans = local // LANES
    for c in range(2):
        flat = jnp.concatenate(
            [every[:, c, a * LANES : (a + 1) * LANES] for a in range(spans)], axis=0
        ).T - 0.5
        high, low = halves(flat)
        table[c * LANES : (c + 1) * LANES, :] = jnp.concatenate([high, low], axis=1)

    def points_of(order):
        length = order.shape[1]
        owner = order // LANES % spans * n + order // local
        lane = order % LANES
        hot = bf(iota0(n * spans, length) == owner)
        got = jnp.dot(
            table[...], jnp.concatenate([hot, hot], axis=0), preferred_element_type=F32
        )
        mine = iota0(LANES, length) == lane
        px, py = (
            jnp.sum(
                jnp.where(mine, got[c * LANES : (c + 1) * LANES], 0.0), axis=0, keepdims=True
            )
            for c in range(2)
        )
        right = []
        for part in (px, py):
            a, b = (h.astype(F32) for h in halves(part))
            right += [a, b, a, b, a]
        right += [jnp.ones_like(px)] * 3 + pieces(px * px + py * py + DELTA_SQUARED)
        return jnp.concatenate(right, axis=0).astype(BF16)

    sources = src_ref.shape[1]

    def block(points, chunk):
        def squares(at):
            return jnp.dot(
                src_left[at : at + chunk, :], points, preferred_element_type=F32
            )

        total = None
        ahead = squares(0)
        for at in range(0, sources, chunk):
            now = ahead
            if at + chunk < sources:
                ahead = squares(at + chunk)
            panel = ((-0.5 * LN2) * jnp.log2(now)).astype(BF16)
            term = jnp.dot(
                om_ref[:, at : at + chunk], panel, preferred_element_type=F32
            )
            total = term if total is None else total + term
        return total

    class Stream:
        def __init__(self, refs):
            self.own, self.part_out, self.part_in, self.z_out, self.z_in = refs[:5]
            self.sems = refs[5:]

        def keep(self, x, theirs, mine):
            self.part_out[x] = theirs
            self.part_copy(x).start()
            self.own[x] = mine

        def part_copy(self, x):
            return pltpu.make_async_remote_copy(
                src_ref=self.part_out.at[x], dst_ref=self.part_in.at[x],
                send_sem=self.sems[0].at[x], recv_sem=self.sems[1].at[x],
                device_id=(row, partner), device_id_type=MESH,
            )

        def z_copy(self, x, b):
            return pltpu.make_async_remote_copy(
                src_ref=self.z_out.at[x], dst_ref=self.z_in.at[x],
                send_sem=self.sems[2].at[x], recv_sem=self.sems[3].at[x],
                device_id=(row, flip(z, 2**b, bits) * 2 + core), device_id_type=MESH,
            )

        def total(self, x):
            low = bits if x == 0 else (x & -x).bit_length() - 1
            self.part_copy(x).wait()
            out = self.own[x] + self.part_in[x]
            for b in range(low):
                self.z_copy(x + 2**b, b).wait()
                out = out + self.z_in[x + 2**b].astype(F32)
            return out

        def pass_on(self, x):
            self.z_out[x] = self.total(x).astype(BF16)
            self.z_copy(x, (x & -x).bit_length() - 1).start()

    edge = k + streamed[STREAM_REFS].shape[2]
    spans_of = {"A": slice(0, k), "B": slice(k, edge), "C": slice(edge, length)}
    streams = {
        name: Stream(streamed[i * STREAM_REFS : (i + 1) * STREAM_REFS])
        for i, name in enumerate("ABC")
    }

    def parts_of(step):
        return [(step[i], int(step[i + 1])) for i in range(0, len(step), 2)]

    def points_for(step):
        chosen = []
        for name, x in parts_of(step):
            to = flip(z, x, bits)
            for leaf in (to * 2 + (1 - core), to * 2 + core):
                chosen.append(orders[leaf][:, spans_of[name]])
        return points_of(jnp.concatenate(chosen, axis=1))

    def compute(step, points):
        total = block(points, min(CHUNK, points.shape[1]))
        at = 0
        for name, x in parts_of(step):
            size = spans_of[name].stop - spans_of[name].start
            streams[name].keep(
                x, total[:, at : at + size], total[:, at + size : at + 2 * size]
            )
            at += 2 * size

    near = pltpu.make_async_remote_copy(
        src_ref=near_out, dst_ref=near_in, send_sem=near_send, recv_sem=near_recv,
        device_id=(row, partner), device_id_type=MESH,
    )
    half = far_out.shape[0] // 2
    share = pl.ds(pl.multiple_of(core * half, half), half)

    def far_copy(m):
        return pltpu.make_async_remote_copy(
            src_ref=far_out.at[share], dst_ref=far_in.at[m - 1, share],
            send_sem=far_send.at[m - 1], recv_sem=far_recv.at[m - 1],
            device_id=(row, flip(z, m, bits) * 2 + core), device_id_type=MESH,
        )

    def pass_copy(m):
        return pltpu.make_async_remote_copy(
            src_ref=far_in.at[m - 1, share], dst_ref=far_in.at[m - 1, share],
            send_sem=pass_send.at[m - 1], recv_sem=pass_recv.at[m - 1],
            device_id=(row, partner), device_id_type=MESH,
        )

    def hot_of(table, node, side):
        return bf(iota0(k, k) + side * k == table[pl.ds(node, 1), :])

    def offer_near():
        ch_ref[0] = streams["A"].total(0)
        near_out[...] = ch_ref[0]
        near.start()

    def accept_near():
        own = pick(split3(ch_ref[0]), hot_of(p1_ref, me // 2, core))
        hot = hot_of(p1_ref, me // 2, 1 - core)
        near.wait()
        ch_ref[1] = own + pick(split3(near_in[...]), hot)
        far_out[...] = ch_ref[1].astype(BF16)
        for m in range(1, GROUP):
            far_copy(m).start()

    def relay():
        for m in range(1, GROUP):
            far_copy(m).wait()
            pass_copy(m).start()

    def accept_far():
        node = me // 4
        sibling = node + 1 - 2 * (node % 2)
        low, high = z % 2, z // 2 % 2
        near_pair = [hot_of(p2_ref, node, s) for s in (low, 1 - low)]
        far_pair = [hot_of(p2_ref, sibling, s) for s in (low, 1 - low)]
        tops = [hot_of(p3_ref, me // 8, s) for s in (high, 1 - high)]

        def through(hot, top):
            return jnp.dot(hot, top, preferred_element_type=F32).astype(BF16)

        none = jnp.zeros_like(tops[0])
        rows = [
            [hot, through(hot, tops[0])] for hot in near_pair
        ] + [[none, through(hot, tops[1])] for hot in far_pair]
        rows = [jnp.concatenate(r, axis=1) for r in rows]
        own = pick(split3(ch_ref[1]), rows[0])
        hot = jnp.concatenate(rows[1:], axis=0)
        for m in range(1, GROUP):
            pass_copy(m).wait()
        theirs = jnp.concatenate([far_in[m - 1] for m in range(1, GROUP)], axis=1)
        both = own + jnp.dot(theirs, hot, preferred_element_type=F32)
        ch_ref[2] = both[:, :k]
        ch_ref[3] = both[:, k:]

    seq = []
    for b in range(bits):
        count = zs // 2 ** (b + 1)
        seq += [(2 * (count - 1 - j) + 1) * 2**b for j in range(count)]
    seq.append(0)

    if zs == 4:
        plan = " ".join(PLAN).split()
    else:
        plan = []
        for names in ("AB", "C"):
            for i, x in enumerate(seq):
                plan.append("".join(f"{name}{x}" for name in names))
                plan += [f"p{name}{y}" for y in seq[i - 1 : i] for name in names]
        plan += ["o0", "a0", "i0", "r0", "a1"]

    def interpolate(s, o_ref, inv):
        r_ref[...] = contract0(ch_ref[s], ch_ref[s + 1])
        size = o_ref.shape[0]
        at = pl.multiple_of(col % 2**s * size, size)
        o_ref[...] = product6(r_ref[pl.ds(at, size), :], inv)

    def solve_low():
        grams = [contract0(ch_ref[m], ch_ref[m]) for m in range(2)]
        inverse = shifted_inverses(grams)
        g_ref[...] = lax.dot_general(
            inverse[0], ch_ref[0], (((0,), (1,)), ((), ())),
            precision=HIGHEST, preferred_element_type=F32,
        )
        base_ref[...] = placed(base_place, product6(grams[0], inverse[0]))
        interpolate(0, o1_ref, inverse[1])

    steps = {
        "o0": offer_near, "a0": accept_near, "r0": relay, "i0": solve_low, "a1": accept_far
    }
    blocks = [step for step in plan if step[0] in "ABC"]
    points = points_for(blocks[0])
    for step in plan:
        if step in steps:
            steps[step]()
        elif step[0] == "p":
            streams[step[1]].pass_on(int(step[2:]))
        else:
            now = points
            blocks = blocks[1:]
            if blocks:
                points = points_for(blocks[0])
            compute(step, now)
    inverse = shifted_inverses([contract0(ch_ref[m], ch_ref[m]) for m in (2, 3)])
    t_ref[...] = ch_ref[3].T
    size = root_ref.shape[0]
    root_ref[...] = t_ref[pl.ds(pl.multiple_of(col % 2**LEVELS * size, size), size), :]
    interpolate(1, o2_ref, inverse[0])
    interpolate(2, o3_ref, inverse[1])
    rest_ref[:, : edge - k] = streams["B"].total(0)
    rest_ref[:, edge - k :] = streams["C"].total(0)


def placed(place, x):
    high, low = halves(x)
    both = jnp.dot(
        place, jnp.concatenate([high, low], axis=1), preferred_element_type=F32
    )
    return both[:, : x.shape[1]] + both[:, x.shape[1] :]


def contract0(a, b):
    return lax.dot_general(
        a, b, (((0,), (0,)), ((), ())), precision=HIGHEST, preferred_element_type=F32
    )


def halves(x):
    h = x.astype(BF16)
    return h, (x - h.astype(F32)).astype(BF16)


def product4(a, b):
    k = b.shape[1]
    right = jnp.concatenate(halves(b), axis=1)
    both = jnp.dot(
        jnp.concatenate(halves(a), axis=1),
        jnp.concatenate([right, right], axis=0),
        preferred_element_type=F32,
    )
    return both[:, :k] + both[:, k:]


def product6(a, b):
    return jnp.dot(a, b, precision=HIGHEST, preferred_element_type=F32)


def shifted_inverses(grams):
    k = grams[0].shape[0]
    eye = lax.broadcasted_iota(jnp.int32, (k, k), 0) == lax.broadcasted_iota(
        jnp.int32, (k, k), 1
    )
    one = jnp.where(eye, 1.0, 0.0)
    low = 1.0 / (k / RIDGE + 1.0)
    gap = (1.0 - low) / (1.0 + low)
    first = 2.0 / (1.0 + low)
    tops, mats = [], []
    for gram in grams:
        trace = jnp.sum(jnp.where(eye, gram, 0.0), axis=(0, 1), keepdims=True)
        shift = RIDGE * (trace / k + 1e-06)
        tops.append(trace + shift)
        mats.append((gram + shift * one) / (trace + shift))
    scale = 2.0 / (2.0 - gap * gap)
    xs = [scale * (2.0 * first * one - first * first * m) for m in mats]
    gap = gap * gap / (2.0 - gap * gap)
    scales = []
    while gap > 2e-6:
        scales.append(2.0 / (2.0 - gap * gap))
        gap = gap * gap / (2.0 - gap * gap)
    pairs = [jnp.concatenate([product4(m, x), x], axis=0) for m, x in zip(mats, xs)]
    for scale in scales[:-2]:
        ys = [scale * (2.0 * one - pair[:k]) for pair in pairs]
        pairs = [product4(pair, y) for pair, y in zip(pairs, ys)]
    xs = [pair[k:] for pair in pairs]
    for scale in scales[-2:]:
        ys = [scale * (2.0 * one - product6(m, x)) for m, x in zip(mats, xs)]
        xs = [product4(x, y) for x, y in zip(xs, ys)]
    return [x / t for x, t in zip(xs, tops)]


def solve_kernel(
    rest_ref, g_ref, base_ref, place_ref, i1, i2, i3, top, o0, o1, o2, o3, root
):
    for got, o in ((i1, o1), (i2, o2), (i3, o3), (top, root)):
        o[...] = got[...]
    g, g_low = halves(g_ref[...])
    rest, rest_low = halves(rest_ref[...])
    dot = functools.partial(jnp.dot, preferred_element_type=F32)
    rows = dot(g, rest) + (dot(g, rest_low) + dot(g_low, rest))
    moved = lax.dot_general(
        place_ref[...], jnp.concatenate(halves(rows), axis=0), (((1,), (1,)), ((), ())),
        preferred_element_type=F32,
    )
    k = o0.shape[1]
    o0[...] = base_ref[...] + (moved[:, :k] + moved[:, k:])


def body(rows, cols, targets, sources, omega, tree_order, leaf_pivots, p1, p2, p3):
    n = rows * cols
    zs = cols // 2
    leaf = tree_order.shape[0]
    width = omega.shape[0]
    k = leaf_pivots.shape[1]
    rest = leaf - k
    spans = targets.shape[1] // LANES
    vmem = pl.BlockSpec(memory_space=pltpu.VMEM)
    hbm = pl.BlockSpec(memory_space=pltpu.HBM)
    dma = lambda *d: pltpu.SemaphoreType.DMA(d)
    held = lambda a: pltpu.VMEM(a.shape, a.dtype)
    order = tree_order.reshape(1, leaf)

    def stream(size):
        wide, narrow = (pltpu.VMEM((zs, width, size), t) for t in (F32, BF16))
        return [wide, wide, wide, narrow, narrow] + [dma(zs)] * 4

    out_rows = [leaf] + [k // 2**s for s in range(LEVELS)]
    kept = pl.pallas_call(
        functools.partial(sketch_kernel, rows, cols),
        out_shape=(
            pltpu.VMEM((width, rest), F32),
            pltpu.VMEM((k, width), F32),
            pltpu.VMEM((leaf, k), F32),
            pltpu.VMEM((leaf, rest), BF16),
        )
        + tuple(pltpu.VMEM((r, k), F32) for r in out_rows[1:])
        + (pltpu.VMEM((k // 2**LEVELS, width), F32),),
        in_specs=[hbm] * 8,
        out_specs=(vmem,) * (LEVELS + 5),
        scratch_shapes=[
            held(sources), held(omega), held(order), held(leaf_pivots),
            held(p1), held(p2), held(p3),
            pltpu.VMEM((n, 2, targets.shape[1]), F32),
            pltpu.VMEM((cols, 1, leaf), jnp.int32),
            pltpu.VMEM((2 * LANES, 2 * n * spans), BF16),
            pltpu.VMEM((sources.shape[1], SIDE), BF16),
            pltpu.VMEM((LEVELS + 1, width, k), F32),
            pltpu.VMEM((k, k), F32),
            pltpu.VMEM((k, width), F32),
            *stream(k), *stream(LANES), *stream(rest - LANES),
            pltpu.VMEM((width, k), F32),
            pltpu.VMEM((width, k), F32),
            pltpu.VMEM((width, k), BF16),
            pltpu.VMEM((GROUP - 1, width, k), BF16),
            dma(8),
            *[pltpu.SemaphoreType.DMA] * 6,
            *[dma(GROUP - 1)] * 4,
        ],
        compiler_params=pltpu.CompilerParams(
            collective_id=0, has_side_effects=True, vmem_limit_bytes=60 << 20
        ),
    )(targets, sources, omega, order, leaf_pivots, p1, p2, p3)
    return pl.pallas_call(
        solve_kernel,
        out_shape=tuple(jax.ShapeDtypeStruct((r, k), F32) for r in out_rows)
        + (jax.ShapeDtypeStruct((k // 2**LEVELS, width), F32),),
        in_specs=[vmem] * len(kept),
        out_specs=(vmem,) * (len(out_rows) + 1),
        compiler_params=pltpu.CompilerParams(vmem_limit_bytes=32 << 20),
    )(*kept)


def solution(mesh):
    both = P(("row", "col"), None)
    return jax.shard_map(
        functools.partial(body, mesh.shape["row"], mesh.shape["col"]),
        mesh=mesh,
        in_specs=(
            P(None, ("row", "col")),
            P(None, "col"),
            P(None, "col"),
            P(("row", "col")),
            both,
            P(),
            P(),
            P(),
        ),
        out_specs=(both,) * 5,
        check_vma=False,
    )
```

```python
import functools

import jax
import jax.numpy as jnp
from jax import lax
from jax.experimental import pallas as pl
from jax.experimental.pallas import tpu as pltpu
from jax.sharding import PartitionSpec as P

RIDGE = 0.1
DELTA_SQUARED = 0.0001
LEVELS = 3
LANES = 128
CHUNK = 512
SIDE = 16
STREAM_REFS = 9
PLAN = (
    "A3B3", "A1B1", "pA3", "A2B2", "pA1", "A0B0", "pA2", "C3",
    "pB3", "C2", "pC3", "o0", "C1", "a0", "C0", "pB2",
    "pC2", "pB1", "pC1", "i0", "r0", "a1",
)
GROUP = 2 ** (LEVELS - 1)
LN2 = 0.6931471805599453
MESH = pl.DeviceIdType.MESH
HIGHEST = lax.Precision.HIGHEST
F32 = jnp.float32
BF16 = jnp.bfloat16


def split3(x):
    a = x.astype(BF16)
    r = x - a.astype(F32)
    b = r.astype(BF16)
    c = (r - b.astype(F32)).astype(BF16)
    return a, b, c


def pick(parts, hot):
    out = None
    for part in parts:
        term = jnp.dot(part, hot, preferred_element_type=F32)
        out = term if out is None else out + term
    return out


def flip(value, mask, bits):
    out = 0
    for i in range(bits):
        out = out + (value // 2**i + mask // 2**i) % 2 * 2**i
    return out


def sketch_kernel(
    rows, cols,
    tgt_hbm, src_hbm, om_hbm, ord_hbm, leaf_hbm, p1_hbm, p2_hbm, p3_hbm,
    rest_ref, g_ref, base_ref, place_ref, o1_ref, o2_ref, o3_ref, root_ref,
    src_ref, om_ref, raw_ref, leaf_ref, p1_ref, p2_ref, p3_ref,
    every, orders, table, src_left, ch_ref, r_ref, t_ref,
    *scratch,
):
    streamed, scratch = scratch[: 3 * STREAM_REFS], scratch[3 * STREAM_REFS :]
    (
        near_out, near_in, far_out, far_in, load_sem, tgt_send, tgt_recv, ord_send, ord_recv,
        near_send, near_recv, far_send, far_recv, pass_send, pass_recv,
    ) = scratch
    n = rows * cols
    zs = cols // 2
    bits = zs.bit_length() - 1
    row = lax.axis_index("row")
    col = lax.axis_index("col")
    me = row * cols + col
    z = col // 2
    core = col % 2
    partner = z * 2 + (1 - core)
    length = ord_hbm.shape[1]
    local = tgt_hbm.shape[1]
    k = leaf_hbm.shape[1]
    rest = length - k

    def load_of(i, src, dst):
        return pltpu.make_async_copy(src, dst, load_sem.at[i])

    early = [
        load_of(0, ord_hbm, raw_ref), load_of(1, leaf_hbm, leaf_ref),
        load_of(2, src_hbm, src_ref), load_of(3, tgt_hbm, every.at[me]),
    ]
    later = [
        load_of(4, om_hbm, om_ref), load_of(5, p1_hbm, p1_ref),
        load_of(6, p2_hbm, p2_ref), load_of(7, p3_hbm, p3_ref),
    ]
    for load in early + later:
        load.start()

    barrier = pltpu.get_barrier_semaphore()

    def away(mask):
        out_row, out_col = row, col
        for b in range((cols - 1).bit_length()):
            if mask >> b & 1:
                out_col = out_col + (1 - 2 * (col // 2**b % 2)) * 2**b
        for b in range((rows - 1).bit_length()):
            if mask // cols >> b & 1:
                out_row = out_row + (1 - 2 * (row // 2**b % 2)) * 2**b
        return out_row, out_col

    def for_others(go):
        if n <= 64:
            for mask in range(n - 1, 0, -1):
                go(away(mask))
        else:

            def step(i, carry):
                other = lax.rem(me + i, n)
                go((other // cols, other % cols))
                return carry

            lax.fori_loop(1, n, step, 0)

    def greet(device):
        pl.semaphore_signal(barrier, inc=1, device_id=device, device_id_type=MESH)

    for_others(greet)

    def pieces(x):
        return [p.astype(F32) for p in split3(x)]

    for load in early:
        load.wait()

    iota0 = lambda *d: lax.broadcasted_iota(jnp.int32, d, 0)
    iota1 = lambda *d: lax.broadcasted_iota(jnp.int32, d, 1)
    bf = lambda mask: mask.astype(F32).astype(BF16)

    is_pivot = (iota0(length, k) == leaf_ref[...]).astype(F32)
    taken = jnp.sum(is_pivot, axis=1, keepdims=True)
    at = jnp.sum(is_pivot * iota1(length, k).astype(F32), axis=1, keepdims=True)
    free = jnp.broadcast_to(1.0 - taken, (length, LANES)).astype(BF16)
    rank = jnp.dot(
        bf(iota1(length, length) < iota0(length, length)), free, preferred_element_type=F32
    )[:, 0:1]
    slot = jnp.where(taken > 0.5, at, rank + k)
    place = bf(slot == iota1(length, length).astype(F32))
    place_ref[...] = place[:, k:]
    base_place = place[:, :k]
    raw = raw_ref[...]
    digits = jnp.concatenate(
        [raw % 128, raw // 128 % 128, raw // 16384] + [jnp.zeros_like(raw)] * 5, axis=0
    ).astype(F32).astype(BF16)
    moved = jnp.dot(digits, place, preferred_element_type=F32)
    orders[col] = (moved[0:1] + 128.0 * moved[1:2] + 16384.0 * moved[2:3]).astype(jnp.int32)

    wide = src_ref[...].astype(F32) - 0.5
    sx, sy = wide[0:1], wide[1:2]
    ones = jnp.ones_like(sx)
    left = []
    for part in (-2.0 * sx, -2.0 * sy):
        a, b, c = pieces(part)
        left += [a, a, b, b, c]
    left += pieces(sx * sx + sy * sy) + [ones] * 3
    src_left[...] = jnp.concatenate(left, axis=0).T.astype(BF16)

    pl.semaphore_wait(barrier, n - 1)

    def tgt_copy(device, src, dst):
        return pltpu.make_async_remote_copy(
            src_ref=src, dst_ref=dst, send_sem=tgt_send, recv_sem=tgt_recv,
            device_id=device, device_id_type=MESH,
        )

    def ord_copy(device, src, dst):
        return pltpu.make_async_remote_copy(
            src_ref=src, dst_ref=dst, send_sem=ord_send, recv_sem=ord_recv,
            device_id=device, device_id_type=MESH,
        )

    for_others(lambda device: tgt_copy(device, tgt_hbm, every.at[me]).start())
    for mask in range(cols - 1, 0, -1):
        ord_copy(away(mask), orders.at[col], orders.at[col]).start()
    for load in later:
        load.wait()
    whole = every.at[pl.ds(0, n - 1)]
    tgt_copy((row, partner), whole, whole).wait()
    whole = orders.at[pl.ds(0, cols - 1)]
    ord_copy((row, partner), whole, whole).wait()

    spans = local // LANES
    for c in range(2):
        flat = jnp.concatenate(
            [every[:, c, a * LANES : (a + 1) * LANES] for a in range(spans)], axis=0
        ).T - 0.5
        high, low = halves(flat)
        table[c * LANES : (c + 1) * LANES, :] = jnp.concatenate([high, low], axis=1)

    def points_of(order):
        length = order.shape[1]
        owner = order // LANES % spans * n + order // local
        lane = order % LANES
        hot = bf(iota0(n * spans, length) == owner)
        got = jnp.dot(
            table[...], jnp.concatenate([hot, hot], axis=0), preferred_element_type=F32
        )
        mine = iota0(LANES, length) == lane
        px, py = (
            jnp.sum(
                jnp.where(mine, got[c * LANES : (c + 1) * LANES], 0.0), axis=0, keepdims=True
            )
            for c in range(2)
        )
        right = []
        for part in (px, py):
            a, b = (h.astype(F32) for h in halves(part))
            right += [a, b, a, b, a]
        right += [jnp.ones_like(px)] * 3 + pieces(px * px + py * py + DELTA_SQUARED)
        return jnp.concatenate(right, axis=0).astype(BF16)

    sources = src_ref.shape[1]

    def block(points, chunk):
        def squares(at):
            return jnp.dot(
                src_left[at : at + chunk, :], points, preferred_element_type=F32
            )

        total = None
        ahead = squares(0)
        for at in range(0, sources, chunk):
            now = ahead
            if at + chunk < sources:
                ahead = squares(at + chunk)
            panel = ((-0.5 * LN2) * jnp.log2(now)).astype(BF16)
            term = jnp.dot(
                om_ref[:, at : at + chunk], panel, preferred_element_type=F32
            )
            total = term if total is None else total + term
        return total

    class Stream:
        def __init__(self, refs):
            self.own, self.part_out, self.part_in, self.z_out, self.z_in = refs[:5]
            self.sems = refs[5:]

        def keep(self, x, theirs, mine):
            self.part_out[x] = theirs
            self.part_copy(x).start()
            self.own[x] = mine

        def part_copy(self, x):
            return pltpu.make_async_remote_copy(
                src_ref=self.part_out.at[x], dst_ref=self.part_in.at[x],
                send_sem=self.sems[0].at[x], recv_sem=self.sems[1].at[x],
                device_id=(row, partner), device_id_type=MESH,
            )

        def z_copy(self, x, b):
            return pltpu.make_async_remote_copy(
                src_ref=self.z_out.at[x], dst_ref=self.z_in.at[x],
                send_sem=self.sems[2].at[x], recv_sem=self.sems[3].at[x],
                device_id=(row, flip(z, 2**b, bits) * 2 + core), device_id_type=MESH,
            )

        def total(self, x):
            low = bits if x == 0 else (x & -x).bit_length() - 1
            self.part_copy(x).wait()
            out = self.own[x] + self.part_in[x]
            for b in range(low):
                self.z_copy(x + 2**b, b).wait()
                out = out + self.z_in[x + 2**b].astype(F32)
            return out

        def pass_on(self, x):
            self.z_out[x] = self.total(x).astype(BF16)
            self.z_copy(x, (x & -x).bit_length() - 1).start()

    edge = k + streamed[STREAM_REFS].shape[2]
    spans_of = {"A": slice(0, k), "B": slice(k, edge), "C": slice(edge, length)}
    streams = {
        name: Stream(streamed[i * STREAM_REFS : (i + 1) * STREAM_REFS])
        for i, name in enumerate("ABC")
    }

    def parts_of(step):
        return [(step[i], int(step[i + 1])) for i in range(0, len(step), 2)]

    def points_for(step):
        chosen = []
        for name, x in parts_of(step):
            to = flip(z, x, bits)
            for leaf in (to * 2 + (1 - core), to * 2 + core):
                chosen.append(orders[leaf][:, spans_of[name]])
        return points_of(jnp.concatenate(chosen, axis=1))

    def compute(step, points):
        total = block(points, min(CHUNK, points.shape[1]))
        at = 0
        for name, x in parts_of(step):
            size = spans_of[name].stop - spans_of[name].start
            streams[name].keep(
                x, total[:, at : at + size], total[:, at + size : at + 2 * size]
            )
            at += 2 * size

    near = pltpu.make_async_remote_copy(
        src_ref=near_out, dst_ref=near_in, send_sem=near_send, recv_sem=near_recv,
        device_id=(row, partner), device_id_type=MESH,
    )
    half = far_out.shape[0] // 2
    share = pl.ds(pl.multiple_of(core * half, half), half)

    def far_copy(m):
        return pltpu.make_async_remote_copy(
            src_ref=far_out.at[share], dst_ref=far_in.at[m - 1, share],
            send_sem=far_send.at[m - 1], recv_sem=far_recv.at[m - 1],
            device_id=(row, flip(z, m, bits) * 2 + core), device_id_type=MESH,
        )

    def pass_copy(m):
        return pltpu.make_async_remote_copy(
            src_ref=far_in.at[m - 1, share], dst_ref=far_in.at[m - 1, share],
            send_sem=pass_send.at[m - 1], recv_sem=pass_recv.at[m - 1],
            device_id=(row, partner), device_id_type=MESH,
        )

    def hot_of(table, node, side):
        return bf(iota0(k, k) + side * k == table[pl.ds(node, 1), :])

    def offer_near():
        ch_ref[0] = streams["A"].total(0)
        near_out[...] = ch_ref[0]
        near.start()

    def accept_near():
        own = pick(split3(ch_ref[0]), hot_of(p1_ref, me // 2, core))
        hot = hot_of(p1_ref, me // 2, 1 - core)
        near.wait()
        ch_ref[1] = own + pick(split3(near_in[...]), hot)
        far_out[...] = ch_ref[1].astype(BF16)
        for m in range(1, GROUP):
            far_copy(m).start()

    def relay():
        for m in range(1, GROUP):
            far_copy(m).wait()
            pass_copy(m).start()

    def accept_far():
        node = me // 4
        sibling = node + 1 - 2 * (node % 2)
        low, high = z % 2, z // 2 % 2
        near_pair = [hot_of(p2_ref, node, s) for s in (low, 1 - low)]
        far_pair = [hot_of(p2_ref, sibling, s) for s in (low, 1 - low)]
        tops = [hot_of(p3_ref, me // 8, s) for s in (high, 1 - high)]

        def through(hot, top):
            return jnp.dot(hot, top, preferred_element_type=F32).astype(BF16)

        none = jnp.zeros_like(tops[0])
        rows = [
            [hot, through(hot, tops[0])] for hot in near_pair
        ] + [[none, through(hot, tops[1])] for hot in far_pair]
        rows = [jnp.concatenate(r, axis=1) for r in rows]
        own = pick(split3(ch_ref[1]), rows[0])
        hot = jnp.concatenate(rows[1:], axis=0)
        for m in range(1, GROUP):
            pass_copy(m).wait()
        theirs = jnp.concatenate([far_in[m - 1] for m in range(1, GROUP)], axis=1)
        both = own + jnp.dot(theirs, hot, preferred_element_type=F32)
        ch_ref[2] = both[:, :k]
        ch_ref[3] = both[:, k:]

    seq = []
    for b in range(bits):
        count = zs // 2 ** (b + 1)
        seq += [(2 * (count - 1 - j) + 1) * 2**b for j in range(count)]
    seq.append(0)

    if zs == 4:
        plan = list(PLAN)
    else:
        plan = []
        for names in ("AB", "C"):
            for i, x in enumerate(seq):
                plan.append("".join(f"{name}{x}" for name in names))
                plan += [f"p{name}{y}" for y in seq[i - 1 : i] for name in names]
        plan += ["o0", "a0", "i0", "r0", "a1"]

    def relate(s, o_ref):
        r_ref[s] = contract0(ch_ref[s], ch_ref[s + 1])
        size = o_ref.shape[0]
        at = pl.multiple_of(col % 2**s * size, size)
        return r_ref[s, pl.ds(at, size), :]

    def solve_low():
        grams = [contract0(ch_ref[m], ch_ref[m]) for m in range(2)]
        related = relate(0, o1_ref)
        inverse = shifted_inverses(grams)
        g_ref[...] = lax.dot_general(
            inverse[0], ch_ref[0], (((0,), (1,)), ((), ())),
            precision=HIGHEST, preferred_element_type=F32,
        )
        base_ref[...] = placed(base_place, product6(grams[0], inverse[0]))
        o1_ref[...] = product6(related, inverse[1])

    steps = {
        "o0": offer_near, "a0": accept_near, "r0": relay, "i0": solve_low, "a1": accept_far
    }
    blocks = [step for step in plan if step[0] in "ABC"]
    points = points_for(blocks[0])
    for step in plan:
        if step in steps:
            steps[step]()
        elif step[0] == "p":
            streams[step[1]].pass_on(int(step[2:]))
        else:
            now = points
            blocks = blocks[1:]
            if blocks:
                points = points_for(blocks[0])
            compute(step, now)
    grams = [contract0(ch_ref[m], ch_ref[m]) for m in (2, 3)]
    related = [relate(1, o2_ref), relate(2, o3_ref)]
    t_ref[...] = ch_ref[3].T
    size = root_ref.shape[0]
    root_ref[...] = t_ref[pl.ds(pl.multiple_of(col % 2**LEVELS * size, size), size), :]
    inverse = shifted_inverses(grams)
    o2_ref[...] = product6(related[0], inverse[0])
    o3_ref[...] = product6(related[1], inverse[1])
    rest_ref[:, : edge - k] = streams["B"].total(0)
    rest_ref[:, edge - k :] = streams["C"].total(0)


def placed(place, x):
    high, low = halves(x)
    both = jnp.dot(
        place, jnp.concatenate([high, low], axis=1), preferred_element_type=F32
    )
    return both[:, : x.shape[1]] + both[:, x.shape[1] :]


def contract0(a, b):
    return lax.dot_general(
        a, b, (((0,), (0,)), ((), ())), precision=HIGHEST, preferred_element_type=F32
    )


def halves(x):
    h = x.astype(BF16)
    return h, (x - h.astype(F32)).astype(BF16)


def product4(a, b):
    k = b.shape[1]
    right = jnp.concatenate(halves(b), axis=1)
    both = jnp.dot(
        jnp.concatenate(halves(a), axis=1),
        jnp.concatenate([right, right], axis=0),
        preferred_element_type=F32,
    )
    return both[:, :k] + both[:, k:]


def product6(a, b):
    return jnp.dot(a, b, precision=HIGHEST, preferred_element_type=F32)


def shifted_inverses(grams):
    k = grams[0].shape[0]
    eye = lax.broadcasted_iota(jnp.int32, (k, k), 0) == lax.broadcasted_iota(
        jnp.int32, (k, k), 1
    )
    one = jnp.where(eye, 1.0, 0.0)
    low = 1.0 / (k / RIDGE + 1.0)
    gap = (1.0 - low) / (1.0 + low)
    first = 2.0 / (1.0 + low)
    tops, mats = [], []
    for gram in grams:
        trace = jnp.sum(jnp.where(eye, gram, 0.0), axis=(0, 1), keepdims=True)
        shift = RIDGE * (trace / k + 1e-06)
        tops.append(trace + shift)
        mats.append((gram + shift * one) / (trace + shift))
    scale = 2.0 / (2.0 - gap * gap)
    xs = [scale * (2.0 * first * one - first * first * m) for m in mats]
    gap = gap * gap / (2.0 - gap * gap)
    scales = []
    while gap > 2e-6:
        scales.append(2.0 / (2.0 - gap * gap))
        gap = gap * gap / (2.0 - gap * gap)
    pairs = [jnp.concatenate([product4(m, x), x], axis=0) for m, x in zip(mats, xs)]
    for scale in scales[:-1]:
        ys = [scale * (2.0 * one - pair[:k]) for pair in pairs]
        pairs = [product4(pair, y) for pair, y in zip(pairs, ys)]
    xs = [pair[k:] for pair in pairs]
    for scale in scales[-1:]:
        ys = [scale * (2.0 * one - product6(m, x)) for m, x in zip(mats, xs)]
        xs = [product4(x, y) for x, y in zip(xs, ys)]
    return [x / t for x, t in zip(xs, tops)]


def solve_kernel(
    rest_ref, g_ref, base_ref, place_ref, i1, i2, i3, top, o0, o1, o2, o3, root
):
    for got, o in ((i1, o1), (i2, o2), (i3, o3), (top, root)):
        o[...] = got[...]
    g, g_low = halves(g_ref[...])
    rest, rest_low = halves(rest_ref[...])
    dot = functools.partial(jnp.dot, preferred_element_type=F32)
    rows = dot(g, rest) + (dot(g, rest_low) + dot(g_low, rest))
    moved = lax.dot_general(
        place_ref[...], jnp.concatenate(halves(rows), axis=0), (((1,), (1,)), ((), ())),
        preferred_element_type=F32,
    )
    k = o0.shape[1]
    o0[...] = base_ref[...] + (moved[:, :k] + moved[:, k:])


def body(rows, cols, targets, sources, omega, tree_order, leaf_pivots, p1, p2, p3):
    n = rows * cols
    zs = cols // 2
    leaf = tree_order.shape[0]
    width = omega.shape[0]
    k = leaf_pivots.shape[1]
    rest = leaf - k
    spans = targets.shape[1] // LANES
    vmem = pl.BlockSpec(memory_space=pltpu.VMEM)
    hbm = pl.BlockSpec(memory_space=pltpu.HBM)
    dma = lambda *d: pltpu.SemaphoreType.DMA(d)
    held = lambda a: pltpu.VMEM(a.shape, a.dtype)
    order = tree_order.reshape(1, leaf)

    def stream(size):
        wide, narrow = (pltpu.VMEM((zs, width, size), t) for t in (F32, BF16))
        return [wide, wide, wide, narrow, narrow] + [dma(zs)] * 4

    out_rows = [leaf] + [k // 2**s for s in range(LEVELS)]
    kept = pl.pallas_call(
        functools.partial(sketch_kernel, rows, cols),
        out_shape=(
            pltpu.VMEM((width, rest), F32),
            pltpu.VMEM((k, width), F32),
            pltpu.VMEM((leaf, k), F32),
            pltpu.VMEM((leaf, rest), BF16),
        )
        + tuple(pltpu.VMEM((r, k), F32) for r in out_rows[1:])
        + (pltpu.VMEM((k // 2**LEVELS, width), F32),),
        in_specs=[hbm] * 8,
        out_specs=(vmem,) * (LEVELS + 5),
        scratch_shapes=[
            held(sources), held(omega), held(order), held(leaf_pivots),
            held(p1), held(p2), held(p3),
            pltpu.VMEM((n, 2, targets.shape[1]), F32),
            pltpu.VMEM((cols, 1, leaf), jnp.int32),
            pltpu.VMEM((2 * LANES, 2 * n * spans), BF16),
            pltpu.VMEM((sources.shape[1], SIDE), BF16),
            pltpu.VMEM((LEVELS + 1, width, k), F32),
            pltpu.VMEM((LEVELS, k, k), F32),
            pltpu.VMEM((k, width), F32),
            *stream(k), *stream(LANES), *stream(rest - LANES),
            pltpu.VMEM((width, k), F32),
            pltpu.VMEM((width, k), F32),
            pltpu.VMEM((width, k), BF16),
            pltpu.VMEM((GROUP - 1, width, k), BF16),
            dma(8),
            *[pltpu.SemaphoreType.DMA] * 6,
            *[dma(GROUP - 1)] * 4,
        ],
        compiler_params=pltpu.CompilerParams(
            collective_id=0, has_side_effects=True, vmem_limit_bytes=60 << 20
        ),
    )(targets, sources, omega, order, leaf_pivots, p1, p2, p3)
    return pl.pallas_call(
        solve_kernel,
        out_shape=tuple(jax.ShapeDtypeStruct((r, k), F32) for r in out_rows)
        + (jax.ShapeDtypeStruct((k // 2**LEVELS, width), F32),),
        in_specs=[vmem] * len(kept),
        out_specs=(vmem,) * (len(out_rows) + 1),
        compiler_params=pltpu.CompilerParams(vmem_limit_bytes=32 << 20),
    )(*kept)


def solution(mesh):
    both = P(("row", "col"), None)
    return jax.shard_map(
        functools.partial(body, mesh.shape["row"], mesh.shape["col"]),
        mesh=mesh,
        in_specs=(
            P(None, ("row", "col")),
            P(None, "col"),
            P(None, "col"),
            P(("row", "col")),
            both,
            P(),
            P(),
            P(),
        ),
        out_specs=(both,) * 5,
        check_vma=False,
    )
```

```python
import functools

import jax
import jax.numpy as jnp
from jax import lax
from jax.experimental import pallas as pl
from jax.experimental.pallas import tpu as pltpu
from jax.sharding import PartitionSpec as P

RIDGE = 0.1
DELTA_SQUARED = 0.0001
LEVELS = 3
LANES = 128
CHUNK = 512
SIDE = 16
STREAM_REFS = 9
PLAN = (
    "A3B3", "C3", "pA3", "A1B1", "pC3", "A2B2", "pA1", "C2",
    "pA2", "A0B0", "pC2", "pB3", "C1", "o0", "C0", "a0",
    "pB1", "i0", "r0", "pC1", "pB2", "a1",
)
GROUP = 2 ** (LEVELS - 1)
LN2 = 0.6931471805599453
MESH = pl.DeviceIdType.MESH
HIGHEST = lax.Precision.HIGHEST
F32 = jnp.float32
BF16 = jnp.bfloat16


def split3(x):
    a = x.astype(BF16)
    r = x - a.astype(F32)
    b = r.astype(BF16)
    c = (r - b.astype(F32)).astype(BF16)
    return a, b, c


def pick(parts, hot):
    out = None
    for part in parts:
        term = jnp.dot(part, hot, preferred_element_type=F32)
        out = term if out is None else out + term
    return out


def flip(value, mask, bits):
    out = 0
    for i in range(bits):
        out = out + (value // 2**i + mask // 2**i) % 2 * 2**i
    return out


def sketch_kernel(
    rows, cols,
    tgt_hbm, src_hbm, om_hbm, ord_hbm, leaf_hbm, p1_hbm, p2_hbm, p3_hbm,
    rest_ref, g_ref, base_ref, place_ref, o1_ref, o2_ref, o3_ref, root_ref,
    src_ref, om_ref, raw_ref, leaf_ref, p1_ref, p2_ref, p3_ref,
    every, orders, table, src_left, ch_ref, r_ref, t_ref,
    *scratch,
):
    streamed, scratch = scratch[: 3 * STREAM_REFS], scratch[3 * STREAM_REFS :]
    (
        near_out, near_in, far_out, far_in, load_sem, tgt_send, tgt_recv, ord_send, ord_recv,
        near_send, near_recv, far_send, far_recv, pass_send, pass_recv,
    ) = scratch
    n = rows * cols
    zs = cols // 2
    bits = zs.bit_length() - 1
    row = lax.axis_index("row")
    col = lax.axis_index("col")
    me = row * cols + col
    z = col // 2
    core = col % 2
    partner = z * 2 + (1 - core)
    length = ord_hbm.shape[1]
    local = tgt_hbm.shape[1]
    k = leaf_hbm.shape[1]
    rest = length - k

    def load_of(i, src, dst):
        return pltpu.make_async_copy(src, dst, load_sem.at[i])

    early = [
        load_of(0, ord_hbm, raw_ref), load_of(1, leaf_hbm, leaf_ref),
        load_of(2, src_hbm, src_ref), load_of(3, tgt_hbm, every.at[me]),
    ]
    later = [
        load_of(4, om_hbm, om_ref), load_of(5, p1_hbm, p1_ref),
        load_of(6, p2_hbm, p2_ref), load_of(7, p3_hbm, p3_ref),
    ]
    for load in early + later:
        load.start()

    barrier = pltpu.get_barrier_semaphore()

    def away(mask):
        out_row, out_col = row, col
        for b in range((cols - 1).bit_length()):
            if mask >> b & 1:
                out_col = out_col + (1 - 2 * (col // 2**b % 2)) * 2**b
        for b in range((rows - 1).bit_length()):
            if mask // cols >> b & 1:
                out_row = out_row + (1 - 2 * (row // 2**b % 2)) * 2**b
        return out_row, out_col

    def for_others(go):
        if n <= 64:
            for mask in range(n - 1, 0, -1):
                go(away(mask))
        else:

            def step(i, carry):
                other = lax.rem(me + i, n)
                go((other // cols, other % cols))
                return carry

            lax.fori_loop(1, n, step, 0)

    def greet(device):
        pl.semaphore_signal(barrier, inc=1, device_id=device, device_id_type=MESH)

    for_others(greet)

    def pieces(x):
        return [p.astype(F32) for p in split3(x)]

    for load in early:
        load.wait()

    iota0 = lambda *d: lax.broadcasted_iota(jnp.int32, d, 0)
    iota1 = lambda *d: lax.broadcasted_iota(jnp.int32, d, 1)
    bf = lambda mask: mask.astype(F32).astype(BF16)

    is_pivot = (iota0(length, k) == leaf_ref[...]).astype(F32)
    taken = jnp.sum(is_pivot, axis=1, keepdims=True)
    at = jnp.sum(is_pivot * iota1(length, k).astype(F32), axis=1, keepdims=True)
    free = jnp.broadcast_to(1.0 - taken, (length, LANES)).astype(BF16)
    rank = jnp.dot(
        bf(iota1(length, length) < iota0(length, length)), free, preferred_element_type=F32
    )[:, 0:1]
    slot = jnp.where(taken > 0.5, at, rank + k)
    place = bf(slot == iota1(length, length).astype(F32))
    place_ref[...] = place[:, k:]
    base_place = place[:, :k]
    raw = raw_ref[...]
    digits = jnp.concatenate(
        [raw % 128, raw // 128 % 128, raw // 16384] + [jnp.zeros_like(raw)] * 5, axis=0
    ).astype(F32).astype(BF16)
    moved = jnp.dot(digits, place, preferred_element_type=F32)
    orders[col] = (moved[0:1] + 128.0 * moved[1:2] + 16384.0 * moved[2:3]).astype(jnp.int32)

    wide = src_ref[...].astype(F32) - 0.5
    sx, sy = wide[0:1], wide[1:2]
    ones = jnp.ones_like(sx)
    left = []
    for part in (-2.0 * sx, -2.0 * sy):
        a, b, c = pieces(part)
        left += [a, a, b, b, c]
    left += pieces(sx * sx + sy * sy) + [ones] * 3
    src_left[...] = jnp.concatenate(left, axis=0).T.astype(BF16)

    pl.semaphore_wait(barrier, n - 1)

    def tgt_copy(device, src, dst):
        return pltpu.make_async_remote_copy(
            src_ref=src, dst_ref=dst, send_sem=tgt_send, recv_sem=tgt_recv,
            device_id=device, device_id_type=MESH,
        )

    def ord_copy(device, src, dst):
        return pltpu.make_async_remote_copy(
            src_ref=src, dst_ref=dst, send_sem=ord_send, recv_sem=ord_recv,
            device_id=device, device_id_type=MESH,
        )

    for_others(lambda device: tgt_copy(device, tgt_hbm, every.at[me]).start())
    for mask in range(cols - 1, 0, -1):
        ord_copy(away(mask), orders.at[col], orders.at[col]).start()
    for load in later:
        load.wait()
    whole = every.at[pl.ds(0, n - 1)]
    tgt_copy((row, partner), whole, whole).wait()
    whole = orders.at[pl.ds(0, cols - 1)]
    ord_copy((row, partner), whole, whole).wait()

    spans = local // LANES
    for c in range(2):
        flat = jnp.concatenate(
            [every[:, c, a * LANES : (a + 1) * LANES] for a in range(spans)], axis=0
        ).T - 0.5
        high, low = halves(flat)
        table[c * LANES : (c + 1) * LANES, :] = jnp.concatenate([high, low], axis=1)

    def points_of(order):
        length = order.shape[1]
        owner = order // LANES % spans * n + order // local
        lane = order % LANES
        hot = bf(iota0(n * spans, length) == owner)
        got = jnp.dot(
            table[...], jnp.concatenate([hot, hot], axis=0), preferred_element_type=F32
        )
        mine = iota0(LANES, length) == lane
        px, py = (
            jnp.sum(
                jnp.where(mine, got[c * LANES : (c + 1) * LANES], 0.0), axis=0, keepdims=True
            )
            for c in range(2)
        )
        right = []
        for part in (px, py):
            a, b = (h.astype(F32) for h in halves(part))
            right += [a, b, a, b, a]
        right += [jnp.ones_like(px)] * 3 + pieces(px * px + py * py + DELTA_SQUARED)
        return jnp.concatenate(right, axis=0).astype(BF16)

    sources = src_ref.shape[1]

    def block(points, chunk):
        def squares(at):
            return jnp.dot(
                src_left[at : at + chunk, :], points, preferred_element_type=F32
            )

        total = None
        ahead = squares(0)
        for at in range(0, sources, chunk):
            now = ahead
            if at + chunk < sources:
                ahead = squares(at + chunk)
            panel = ((-0.5 * LN2) * jnp.log2(now)).astype(BF16)
            term = jnp.dot(
                om_ref[:, at : at + chunk], panel, preferred_element_type=F32
            )
            total = term if total is None else total + term
        return total

    class Stream:
        def __init__(self, refs):
            self.own, self.part_out, self.part_in, self.z_out, self.z_in = refs[:5]
            self.sems = refs[5:]

        def keep(self, x, theirs, mine):
            self.part_out[x] = theirs
            self.part_copy(x).start()
            self.own[x] = mine

        def part_copy(self, x):
            return pltpu.make_async_remote_copy(
                src_ref=self.part_out.at[x], dst_ref=self.part_in.at[x],
                send_sem=self.sems[0].at[x], recv_sem=self.sems[1].at[x],
                device_id=(row, partner), device_id_type=MESH,
            )

        def z_copy(self, x, b):
            return pltpu.make_async_remote_copy(
                src_ref=self.z_out.at[x], dst_ref=self.z_in.at[x],
                send_sem=self.sems[2].at[x], recv_sem=self.sems[3].at[x],
                device_id=(row, flip(z, 2**b, bits) * 2 + core), device_id_type=MESH,
            )

        def total(self, x):
            low = bits if x == 0 else (x & -x).bit_length() - 1
            self.part_copy(x).wait()
            out = self.own[x] + self.part_in[x]
            for b in range(low):
                self.z_copy(x + 2**b, b).wait()
                out = out + self.z_in[x + 2**b].astype(F32)
            return out

        def pass_on(self, x):
            self.z_out[x] = self.total(x).astype(BF16)
            self.z_copy(x, (x & -x).bit_length() - 1).start()

    edge = k + streamed[STREAM_REFS].shape[2]
    spans_of = {"A": slice(0, k), "B": slice(k, edge), "C": slice(edge, length)}
    streams = {
        name: Stream(streamed[i * STREAM_REFS : (i + 1) * STREAM_REFS])
        for i, name in enumerate("ABC")
    }

    def parts_of(step):
        return [(step[i], int(step[i + 1])) for i in range(0, len(step), 2)]

    def points_for(step):
        chosen = []
        for name, x in parts_of(step):
            to = flip(z, x, bits)
            for leaf in (to * 2 + (1 - core), to * 2 + core):
                chosen.append(orders[leaf][:, spans_of[name]])
        return points_of(jnp.concatenate(chosen, axis=1))

    def compute(step, points):
        total = block(points, min(CHUNK, points.shape[1]))
        at = 0
        for name, x in parts_of(step):
            size = spans_of[name].stop - spans_of[name].start
            streams[name].keep(
                x, total[:, at : at + size], total[:, at + size : at + 2 * size]
            )
            at += 2 * size

    near = pltpu.make_async_remote_copy(
        src_ref=near_out, dst_ref=near_in, send_sem=near_send, recv_sem=near_recv,
        device_id=(row, partner), device_id_type=MESH,
    )
    half = far_out.shape[0] // 2
    share = pl.ds(pl.multiple_of(core * half, half), half)

    def far_copy(m):
        return pltpu.make_async_remote_copy(
            src_ref=far_out.at[share], dst_ref=far_in.at[m - 1, share],
            send_sem=far_send.at[m - 1], recv_sem=far_recv.at[m - 1],
            device_id=(row, flip(z, m, bits) * 2 + core), device_id_type=MESH,
        )

    def pass_copy(m):
        return pltpu.make_async_remote_copy(
            src_ref=far_in.at[m - 1, share], dst_ref=far_in.at[m - 1, share],
            send_sem=pass_send.at[m - 1], recv_sem=pass_recv.at[m - 1],
            device_id=(row, partner), device_id_type=MESH,
        )

    def hot_of(table, node, side):
        return bf(iota0(k, k) + side * k == table[pl.ds(node, 1), :])

    def offer_near():
        ch_ref[0] = streams["A"].total(0)
        near_out[...] = ch_ref[0]
        near.start()

    def accept_near():
        own = pick(split3(ch_ref[0]), hot_of(p1_ref, me // 2, core))
        hot = hot_of(p1_ref, me // 2, 1 - core)
        near.wait()
        ch_ref[1] = own + pick(split3(near_in[...]), hot)
        far_out[...] = ch_ref[1].astype(BF16)
        for m in range(1, GROUP):
            far_copy(m).start()

    def relay():
        for m in range(1, GROUP):
            far_copy(m).wait()
            pass_copy(m).start()

    def accept_far():
        node = me // 4
        sibling = node + 1 - 2 * (node % 2)
        low, high = z % 2, z // 2 % 2
        near_pair = [hot_of(p2_ref, node, s) for s in (low, 1 - low)]
        far_pair = [hot_of(p2_ref, sibling, s) for s in (low, 1 - low)]
        tops = [hot_of(p3_ref, me // 8, s) for s in (high, 1 - high)]

        def through(hot, top):
            return jnp.dot(hot, top, preferred_element_type=F32).astype(BF16)

        none = jnp.zeros_like(tops[0])
        rows = [
            [hot, through(hot, tops[0])] for hot in near_pair
        ] + [[none, through(hot, tops[1])] for hot in far_pair]
        rows = [jnp.concatenate(r, axis=1) for r in rows]
        own = pick(split3(ch_ref[1]), rows[0])
        hot = jnp.concatenate(rows[1:], axis=0)
        for m in range(1, GROUP):
            pass_copy(m).wait()
        theirs = jnp.concatenate([far_in[m - 1] for m in range(1, GROUP)], axis=1)
        both = own + jnp.dot(theirs, hot, preferred_element_type=F32)
        ch_ref[2] = both[:, :k]
        ch_ref[3] = both[:, k:]

    seq = []
    for b in range(bits):
        count = zs // 2 ** (b + 1)
        seq += [(2 * (count - 1 - j) + 1) * 2**b for j in range(count)]
    seq.append(0)

    if zs == 4:
        plan = list(PLAN)
    else:
        plan = []
        for names in ("AB", "C"):
            for i, x in enumerate(seq):
                plan.append("".join(f"{name}{x}" for name in names))
                plan += [f"p{name}{y}" for y in seq[i - 1 : i] for name in names]
        plan += ["o0", "a0", "i0", "r0", "a1"]

    def interpolate(s, o_ref, inv):
        r_ref[...] = contract0(ch_ref[s], ch_ref[s + 1])
        size = o_ref.shape[0]
        at = pl.multiple_of(col % 2**s * size, size)
        o_ref[...] = product6(r_ref[pl.ds(at, size), :], inv)

    def solve_low():
        grams = [contract0(ch_ref[m], ch_ref[m]) for m in range(2)]
        inverse = shifted_inverses(grams)
        g_ref[...] = lax.dot_general(
            inverse[0], ch_ref[0], (((0,), (1,)), ((), ())),
            precision=HIGHEST, preferred_element_type=F32,
        )
        base_ref[...] = placed(base_place, product6(grams[0], inverse[0]))
        interpolate(0, o1_ref, inverse[1])

    steps = {
        "o0": offer_near, "a0": accept_near, "r0": relay, "i0": solve_low, "a1": accept_far
    }
    blocks = [step for step in plan if step[0] in "ABC"]
    points = points_for(blocks[0])
    for step in plan:
        if step in steps:
            steps[step]()
        elif step[0] == "p":
            streams[step[1]].pass_on(int(step[2:]))
        else:
            now = points
            blocks = blocks[1:]
            if blocks:
                points = points_for(blocks[0])
            compute(step, now)
    inverse = shifted_inverses([contract0(ch_ref[m], ch_ref[m]) for m in (2, 3)])
    t_ref[...] = ch_ref[3].T
    size = root_ref.shape[0]
    root_ref[...] = t_ref[pl.ds(pl.multiple_of(col % 2**LEVELS * size, size), size), :]
    interpolate(1, o2_ref, inverse[0])
    interpolate(2, o3_ref, inverse[1])
    rest_ref[:, : edge - k] = streams["B"].total(0)
    rest_ref[:, edge - k :] = streams["C"].total(0)


def placed(place, x):
    high, low = halves(x)
    both = jnp.dot(
        place, jnp.concatenate([high, low], axis=1), preferred_element_type=F32
    )
    return both[:, : x.shape[1]] + both[:, x.shape[1] :]


def contract0(a, b):
    return lax.dot_general(
        a, b, (((0,), (0,)), ((), ())), precision=HIGHEST, preferred_element_type=F32
    )


def halves(x):
    h = x.astype(BF16)
    return h, (x - h.astype(F32)).astype(BF16)


def product4(a, b):
    k = b.shape[1]
    right = jnp.concatenate(halves(b), axis=1)
    both = jnp.dot(
        jnp.concatenate(halves(a), axis=1),
        jnp.concatenate([right, right], axis=0),
        preferred_element_type=F32,
    )
    return both[:, :k] + both[:, k:]


def product6(a, b):
    return jnp.dot(a, b, precision=HIGHEST, preferred_element_type=F32)


def shifted_inverses(grams):
    k = grams[0].shape[0]
    eye = lax.broadcasted_iota(jnp.int32, (k, k), 0) == lax.broadcasted_iota(
        jnp.int32, (k, k), 1
    )
    one = jnp.where(eye, 1.0, 0.0)
    low = 1.0 / (k / RIDGE + 1.0)
    gap = (1.0 - low) / (1.0 + low)
    first = 2.0 / (1.0 + low)
    tops, mats = [], []
    for gram in grams:
        trace = jnp.sum(jnp.where(eye, gram, 0.0), axis=(0, 1), keepdims=True)
        shift = RIDGE * (trace / k + 1e-06)
        tops.append(trace + shift)
        mats.append((gram + shift * one) / (trace + shift))
    scale = 2.0 / (2.0 - gap * gap)
    xs = [scale * (2.0 * first * one - first * first * m) for m in mats]
    gap = gap * gap / (2.0 - gap * gap)
    scales = []
    while gap > 2e-6:
        scales.append(2.0 / (2.0 - gap * gap))
        gap = gap * gap / (2.0 - gap * gap)
    pairs = [jnp.concatenate([product4(m, x), x], axis=0) for m, x in zip(mats, xs)]
    for scale in scales[:-2]:
        ys = [scale * (2.0 * one - pair[:k]) for pair in pairs]
        pairs = [product4(pair, y) for pair, y in zip(pairs, ys)]
    xs = [pair[k:] for pair in pairs]
    for scale in scales[-2:]:
        ys = [scale * (2.0 * one - product6(m, x)) for m, x in zip(mats, xs)]
        xs = [product4(x, y) for x, y in zip(xs, ys)]
    return [x / t for x, t in zip(xs, tops)]


def solve_kernel(
    rest_ref, g_ref, base_ref, place_ref, i1, i2, i3, top, o0, o1, o2, o3, root
):
    for got, o in ((i1, o1), (i2, o2), (i3, o3), (top, root)):
        o[...] = got[...]
    g, g_low = halves(g_ref[...])
    rest, rest_low = halves(rest_ref[...])
    dot = functools.partial(jnp.dot, preferred_element_type=F32)
    rows = dot(g, rest) + (dot(g, rest_low) + dot(g_low, rest))
    moved = lax.dot_general(
        place_ref[...], jnp.concatenate(halves(rows), axis=0), (((1,), (1,)), ((), ())),
        preferred_element_type=F32,
    )
    k = o0.shape[1]
    o0[...] = base_ref[...] + (moved[:, :k] + moved[:, k:])


def body(rows, cols, targets, sources, omega, tree_order, leaf_pivots, p1, p2, p3):
    n = rows * cols
    zs = cols // 2
    leaf = tree_order.shape[0]
    width = omega.shape[0]
    k = leaf_pivots.shape[1]
    rest = leaf - k
    spans = targets.shape[1] // LANES
    vmem = pl.BlockSpec(memory_space=pltpu.VMEM)
    hbm = pl.BlockSpec(memory_space=pltpu.HBM)
    dma = lambda *d: pltpu.SemaphoreType.DMA(d)
    held = lambda a: pltpu.VMEM(a.shape, a.dtype)
    order = tree_order.reshape(1, leaf)

    def stream(size):
        wide, narrow = (pltpu.VMEM((zs, width, size), t) for t in (F32, BF16))
        return [wide, wide, wide, narrow, narrow] + [dma(zs)] * 4

    out_rows = [leaf] + [k // 2**s for s in range(LEVELS)]
    kept = pl.pallas_call(
        functools.partial(sketch_kernel, rows, cols),
        out_shape=(
            pltpu.VMEM((width, rest), F32),
            pltpu.VMEM((k, width), F32),
            pltpu.VMEM((leaf, k), F32),
            pltpu.VMEM((leaf, rest), BF16),
        )
        + tuple(pltpu.VMEM((r, k), F32) for r in out_rows[1:])
        + (pltpu.VMEM((k // 2**LEVELS, width), F32),),
        in_specs=[hbm] * 8,
        out_specs=(vmem,) * (LEVELS + 5),
        scratch_shapes=[
            held(sources), held(omega), held(order), held(leaf_pivots),
            held(p1), held(p2), held(p3),
            pltpu.VMEM((n, 2, targets.shape[1]), F32),
            pltpu.VMEM((cols, 1, leaf), jnp.int32),
            pltpu.VMEM((2 * LANES, 2 * n * spans), BF16),
            pltpu.VMEM((sources.shape[1], SIDE), BF16),
            pltpu.VMEM((LEVELS + 1, width, k), F32),
            pltpu.VMEM((k, k), F32),
            pltpu.VMEM((k, width), F32),
            *stream(k), *stream(LANES), *stream(rest - LANES),
            pltpu.VMEM((width, k), F32),
            pltpu.VMEM((width, k), F32),
            pltpu.VMEM((width, k), BF16),
            pltpu.VMEM((GROUP - 1, width, k), BF16),
            dma(8),
            *[pltpu.SemaphoreType.DMA] * 6,
            *[dma(GROUP - 1)] * 4,
        ],
        compiler_params=pltpu.CompilerParams(
            collective_id=0, has_side_effects=True, vmem_limit_bytes=60 << 20
        ),
    )(targets, sources, omega, order, leaf_pivots, p1, p2, p3)
    return pl.pallas_call(
        solve_kernel,
        out_shape=tuple(jax.ShapeDtypeStruct((r, k), F32) for r in out_rows)
        + (jax.ShapeDtypeStruct((k // 2**LEVELS, width), F32),),
        in_specs=[vmem] * len(kept),
        out_specs=(vmem,) * (len(out_rows) + 1),
        compiler_params=pltpu.CompilerParams(vmem_limit_bytes=32 << 20),
    )(*kept)


def solution(mesh):
    both = P(("row", "col"), None)
    return jax.shard_map(
        functools.partial(body, mesh.shape["row"], mesh.shape["col"]),
        mesh=mesh,
        in_specs=(
            P(None, ("row", "col")),
            P(None, "col"),
            P(None, "col"),
            P(("row", "col")),
            both,
            P(),
            P(),
            P(),
        ),
        out_specs=(both,) * 5,
        check_vma=False,
    )
```

```python
import functools

import jax
import jax.numpy as jnp
from jax import lax
from jax.experimental import pallas as pl
from jax.experimental.pallas import tpu as pltpu
from jax.sharding import PartitionSpec as P

RIDGE = 0.1
DELTA_SQUARED = 0.0001
LEVELS = 3
LANES = 128
CHUNK = 512
SIDE = 16
STREAM_REFS = 9
PLAN = (
    "A3B3", "A1B1", "pA3", "A2B2", "pA1", "A0B0", "pA2", "C3",
    "pB3", "C2", "pC3", "pB1", "o0", "C1", "a0", "C0",
    "pB2", "pC2", "pC1", "i0", "r0", "a1",
)
GROUP = 2 ** (LEVELS - 1)
LN2 = 0.6931471805599453
MESH = pl.DeviceIdType.MESH
HIGHEST = lax.Precision.HIGHEST
F32 = jnp.float32
BF16 = jnp.bfloat16


def split3(x):
    a = x.astype(BF16)
    r = x - a.astype(F32)
    b = r.astype(BF16)
    c = (r - b.astype(F32)).astype(BF16)
    return a, b, c


def pick(parts, hot):
    out = None
    for part in parts:
        term = jnp.dot(part, hot, preferred_element_type=F32)
        out = term if out is None else out + term
    return out


def flip(value, mask, bits):
    out = 0
    for i in range(bits):
        out = out + (value // 2**i + mask // 2**i) % 2 * 2**i
    return out


def sketch_kernel(
    rows, cols,
    tgt_hbm, src_hbm, om_hbm, ord_hbm, leaf_hbm, p1_hbm, p2_hbm, p3_hbm,
    rest_ref, g_ref, base_ref, place_ref, o1_ref, o2_ref, o3_ref, root_ref,
    src_ref, om_ref, raw_ref, leaf_ref, p1_ref, p2_ref, p3_ref,
    every, orders, table, src_left, ch_ref, r_ref, t_ref,
    *scratch,
):
    streamed, scratch = scratch[: 3 * STREAM_REFS], scratch[3 * STREAM_REFS :]
    (
        near_out, near_in, far_out, far_in, load_sem, tgt_send, tgt_recv, ord_send, ord_recv,
        near_send, near_recv, far_send, far_recv, pass_send, pass_recv,
    ) = scratch
    n = rows * cols
    zs = cols // 2
    bits = zs.bit_length() - 1
    row = lax.axis_index("row")
    col = lax.axis_index("col")
    me = row * cols + col
    z = col // 2
    core = col % 2
    partner = z * 2 + (1 - core)
    length = ord_hbm.shape[1]
    local = tgt_hbm.shape[1]
    k = leaf_hbm.shape[1]
    rest = length - k

    def load_of(i, src, dst):
        return pltpu.make_async_copy(src, dst, load_sem.at[i])

    early = [
        load_of(0, ord_hbm, raw_ref), load_of(1, leaf_hbm, leaf_ref),
        load_of(2, src_hbm, src_ref), load_of(3, tgt_hbm, every.at[me]),
    ]
    later = [
        load_of(4, om_hbm, om_ref), load_of(5, p1_hbm, p1_ref),
        load_of(6, p2_hbm, p2_ref), load_of(7, p3_hbm, p3_ref),
    ]
    for load in early + later:
        load.start()

    barrier = pltpu.get_barrier_semaphore()

    def away(mask):
        out_row, out_col = row, col
        for b in range((cols - 1).bit_length()):
            if mask >> b & 1:
                out_col = out_col + (1 - 2 * (col // 2**b % 2)) * 2**b
        for b in range((rows - 1).bit_length()):
            if mask // cols >> b & 1:
                out_row = out_row + (1 - 2 * (row // 2**b % 2)) * 2**b
        return out_row, out_col

    def for_others(go):
        if n <= 64:
            for mask in range(n - 1, 0, -1):
                go(away(mask))
        else:

            def step(i, carry):
                other = lax.rem(me + i, n)
                go((other // cols, other % cols))
                return carry

            lax.fori_loop(1, n, step, 0)

    def greet(device):
        pl.semaphore_signal(barrier, inc=1, device_id=device, device_id_type=MESH)

    for_others(greet)

    def pieces(x):
        return [p.astype(F32) for p in split3(x)]

    for load in early:
        load.wait()

    iota0 = lambda *d: lax.broadcasted_iota(jnp.int32, d, 0)
    iota1 = lambda *d: lax.broadcasted_iota(jnp.int32, d, 1)
    bf = lambda mask: mask.astype(F32).astype(BF16)

    is_pivot = (iota0(length, k) == leaf_ref[...]).astype(F32)
    taken = jnp.sum(is_pivot, axis=1, keepdims=True)
    at = jnp.sum(is_pivot * iota1(length, k).astype(F32), axis=1, keepdims=True)
    free = jnp.broadcast_to(1.0 - taken, (length, LANES)).astype(BF16)
    rank = jnp.dot(
        bf(iota1(length, length) < iota0(length, length)), free, preferred_element_type=F32
    )[:, 0:1]
    slot = jnp.where(taken > 0.5, at, rank + k)
    place = bf(slot == iota1(length, length).astype(F32))
    place_ref[...] = place[:, k:]
    base_place = place[:, :k]
    raw = raw_ref[...]
    digits = jnp.concatenate(
        [raw % 128, raw // 128 % 128, raw // 16384] + [jnp.zeros_like(raw)] * 5, axis=0
    ).astype(F32).astype(BF16)
    moved = jnp.dot(digits, place, preferred_element_type=F32)
    orders[col] = (moved[0:1] + 128.0 * moved[1:2] + 16384.0 * moved[2:3]).astype(jnp.int32)

    wide = src_ref[...].astype(F32) - 0.5
    sx, sy = wide[0:1], wide[1:2]
    ones = jnp.ones_like(sx)
    left = []
    for part in (-2.0 * sx, -2.0 * sy):
        a, b, c = pieces(part)
        left += [a, a, b, b, c]
    left += pieces(sx * sx + sy * sy) + [ones] * 3
    src_left[...] = jnp.concatenate(left, axis=0).T.astype(BF16)

    pl.semaphore_wait(barrier, n - 1)

    def tgt_copy(device, src, dst):
        return pltpu.make_async_remote_copy(
            src_ref=src, dst_ref=dst, send_sem=tgt_send, recv_sem=tgt_recv,
            device_id=device, device_id_type=MESH,
        )

    def ord_copy(device, src, dst):
        return pltpu.make_async_remote_copy(
            src_ref=src, dst_ref=dst, send_sem=ord_send, recv_sem=ord_recv,
            device_id=device, device_id_type=MESH,
        )

    for_others(lambda device: tgt_copy(device, tgt_hbm, every.at[me]).start())
    for mask in range(cols - 1, 0, -1):
        ord_copy(away(mask), orders.at[col], orders.at[col]).start()
    for load in later:
        load.wait()
    whole = every.at[pl.ds(0, n - 1)]
    tgt_copy((row, partner), whole, whole).wait()
    whole = orders.at[pl.ds(0, cols - 1)]
    ord_copy((row, partner), whole, whole).wait()

    spans = local // LANES
    for c in range(2):
        flat = jnp.concatenate(
            [every[:, c, a * LANES : (a + 1) * LANES] for a in range(spans)], axis=0
        ).T - 0.5
        high, low = halves(flat)
        table[c * LANES : (c + 1) * LANES, :] = jnp.concatenate([high, low], axis=1)

    def points_of(order):
        length = order.shape[1]
        owner = order // LANES % spans * n + order // local
        lane = order % LANES
        hot = bf(iota0(n * spans, length) == owner)
        got = jnp.dot(
            table[...], jnp.concatenate([hot, hot], axis=0), preferred_element_type=F32
        )
        mine = iota0(LANES, length) == lane
        px, py = (
            jnp.sum(
                jnp.where(mine, got[c * LANES : (c + 1) * LANES], 0.0), axis=0, keepdims=True
            )
            for c in range(2)
        )
        right = []
        for part in (px, py):
            a, b = (h.astype(F32) for h in halves(part))
            right += [a, b, a, b, a]
        right += [jnp.ones_like(px)] * 3 + pieces(px * px + py * py + DELTA_SQUARED)
        return jnp.concatenate(right, axis=0).astype(BF16)

    sources = src_ref.shape[1]

    def block(points, chunk):
        def squares(at):
            return jnp.dot(
                src_left[at : at + chunk, :], points, preferred_element_type=F32
            )

        total = None
        ahead = squares(0)
        for at in range(0, sources, chunk):
            now = ahead
            if at + chunk < sources:
                ahead = squares(at + chunk)
            panel = ((-0.5 * LN2) * jnp.log2(now)).astype(BF16)
            term = jnp.dot(
                om_ref[:, at : at + chunk], panel, preferred_element_type=F32
            )
            total = term if total is None else total + term
        return total

    class Stream:
        def __init__(self, refs):
            self.own, self.part_out, self.part_in, self.z_out, self.z_in = refs[:5]
            self.sems = refs[5:]

        def keep(self, x, theirs, mine):
            self.part_out[x] = theirs
            self.part_copy(x).start()
            self.own[x] = mine

        def part_copy(self, x):
            return pltpu.make_async_remote_copy(
                src_ref=self.part_out.at[x], dst_ref=self.part_in.at[x],
                send_sem=self.sems[0].at[x], recv_sem=self.sems[1].at[x],
                device_id=(row, partner), device_id_type=MESH,
            )

        def z_copy(self, x, b):
            return pltpu.make_async_remote_copy(
                src_ref=self.z_out.at[x], dst_ref=self.z_in.at[x],
                send_sem=self.sems[2].at[x], recv_sem=self.sems[3].at[x],
                device_id=(row, flip(z, 2**b, bits) * 2 + core), device_id_type=MESH,
            )

        def total(self, x):
            low = bits if x == 0 else (x & -x).bit_length() - 1
            self.part_copy(x).wait()
            out = self.own[x] + self.part_in[x]
            for b in range(low):
                self.z_copy(x + 2**b, b).wait()
                out = out + self.z_in[x + 2**b].astype(F32)
            return out

        def pass_on(self, x):
            self.z_out[x] = self.total(x).astype(BF16)
            self.z_copy(x, (x & -x).bit_length() - 1).start()

    edge = k + streamed[STREAM_REFS].shape[2]
    spans_of = {"A": slice(0, k), "B": slice(k, edge), "C": slice(edge, length)}
    streams = {
        name: Stream(streamed[i * STREAM_REFS : (i + 1) * STREAM_REFS])
        for i, name in enumerate("ABC")
    }

    def parts_of(step):
        return [(step[i], int(step[i + 1])) for i in range(0, len(step), 2)]

    def points_for(step):
        chosen = []
        for name, x in parts_of(step):
            to = flip(z, x, bits)
            for leaf in (to * 2 + (1 - core), to * 2 + core):
                chosen.append(orders[leaf][:, spans_of[name]])
        return points_of(jnp.concatenate(chosen, axis=1))

    def compute(step, points):
        total = block(points, min(CHUNK, points.shape[1]))
        at = 0
        for name, x in parts_of(step):
            size = spans_of[name].stop - spans_of[name].start
            streams[name].keep(
                x, total[:, at : at + size], total[:, at + size : at + 2 * size]
            )
            at += 2 * size

    near = pltpu.make_async_remote_copy(
        src_ref=near_out, dst_ref=near_in, send_sem=near_send, recv_sem=near_recv,
        device_id=(row, partner), device_id_type=MESH,
    )
    half = far_out.shape[0] // 2
    share = pl.ds(pl.multiple_of(core * half, half), half)

    def far_copy(m):
        return pltpu.make_async_remote_copy(
            src_ref=far_out.at[share], dst_ref=far_in.at[m - 1, share],
            send_sem=far_send.at[m - 1], recv_sem=far_recv.at[m - 1],
            device_id=(row, flip(z, m, bits) * 2 + core), device_id_type=MESH,
        )

    def pass_copy(m):
        return pltpu.make_async_remote_copy(
            src_ref=far_in.at[m - 1, share], dst_ref=far_in.at[m - 1, share],
            send_sem=pass_send.at[m - 1], recv_sem=pass_recv.at[m - 1],
            device_id=(row, partner), device_id_type=MESH,
        )

    def hot_of(table, node, side):
        return bf(iota0(k, k) + side * k == table[pl.ds(node, 1), :])

    def offer_near():
        ch_ref[0] = streams["A"].total(0)
        near_out[...] = ch_ref[0]
        near.start()

    def accept_near():
        own = pick(split3(ch_ref[0]), hot_of(p1_ref, me // 2, core))
        hot = hot_of(p1_ref, me // 2, 1 - core)
        near.wait()
        ch_ref[1] = own + pick(split3(near_in[...]), hot)
        far_out[...] = ch_ref[1].astype(BF16)
        for m in range(1, GROUP):
            far_copy(m).start()

    def relay():
        for m in range(1, GROUP):
            far_copy(m).wait()
            pass_copy(m).start()

    def accept_far():
        node = me // 4
        sibling = node + 1 - 2 * (node % 2)
        low, high = z % 2, z // 2 % 2
        near_pair = [hot_of(p2_ref, node, s) for s in (low, 1 - low)]
        far_pair = [hot_of(p2_ref, sibling, s) for s in (low, 1 - low)]
        tops = [hot_of(p3_ref, me // 8, s) for s in (high, 1 - high)]

        def through(hot, top):
            return jnp.dot(hot, top, preferred_element_type=F32).astype(BF16)

        none = jnp.zeros_like(tops[0])
        rows = [
            [hot, through(hot, tops[0])] for hot in near_pair
        ] + [[none, through(hot, tops[1])] for hot in far_pair]
        rows = [jnp.concatenate(r, axis=1) for r in rows]
        own = pick(split3(ch_ref[1]), rows[0])
        hot = jnp.concatenate(rows[1:], axis=0)
        for m in range(1, GROUP):
            pass_copy(m).wait()
        theirs = jnp.concatenate([far_in[m - 1] for m in range(1, GROUP)], axis=1)
        both = own + jnp.dot(theirs, hot, preferred_element_type=F32)
        ch_ref[2] = both[:, :k]
        ch_ref[3] = both[:, k:]

    seq = []
    for b in range(bits):
        count = zs // 2 ** (b + 1)
        seq += [(2 * (count - 1 - j) + 1) * 2**b for j in range(count)]
    seq.append(0)

    if zs == 4:
        plan = list(PLAN)
    else:
        plan = []
        for names in ("AB", "C"):
            for i, x in enumerate(seq):
                plan.append("".join(f"{name}{x}" for name in names))
                plan += [f"p{name}{y}" for y in seq[i - 1 : i] for name in names]
        plan += ["o0", "a0", "i0", "r0", "a1"]

    def relate(s, o_ref):
        r_ref[s] = contract0(ch_ref[s], ch_ref[s + 1])
        size = o_ref.shape[0]
        at = pl.multiple_of(col % 2**s * size, size)
        return r_ref[s, pl.ds(at, size), :]

    def solve_low():
        grams = [contract0(ch_ref[m], ch_ref[m]) for m in range(2)]
        related = relate(0, o1_ref)
        inverse = shifted_inverses(grams)
        g_ref[...] = lax.dot_general(
            inverse[0], ch_ref[0], (((0,), (1,)), ((), ())),
            precision=HIGHEST, preferred_element_type=F32,
        )
        base_ref[...] = placed(base_place, product6(grams[0], inverse[0]))
        o1_ref[...] = product6(related, inverse[1])

    steps = {
        "o0": offer_near, "a0": accept_near, "r0": relay, "i0": solve_low, "a1": accept_far
    }
    blocks = [step for step in plan if step[0] in "ABC"]
    points = points_for(blocks[0])
    for step in plan:
        if step in steps:
            steps[step]()
        elif step[0] == "p":
            streams[step[1]].pass_on(int(step[2:]))
        else:
            now = points
            blocks = blocks[1:]
            if blocks:
                points = points_for(blocks[0])
            compute(step, now)
    grams = [contract0(ch_ref[m], ch_ref[m]) for m in (2, 3)]
    related = [relate(1, o2_ref), relate(2, o3_ref)]
    t_ref[...] = ch_ref[3].T
    size = root_ref.shape[0]
    root_ref[...] = t_ref[pl.ds(pl.multiple_of(col % 2**LEVELS * size, size), size), :]
    inverse = shifted_inverses(grams)
    o2_ref[...] = product6(related[0], inverse[0])
    o3_ref[...] = product6(related[1], inverse[1])
    rest_ref[:, : edge - k] = streams["B"].total(0)
    rest_ref[:, edge - k :] = streams["C"].total(0)


def placed(place, x):
    high, low = halves(x)
    both = jnp.dot(
        place, jnp.concatenate([high, low], axis=1), preferred_element_type=F32
    )
    return both[:, : x.shape[1]] + both[:, x.shape[1] :]


def contract0(a, b):
    return lax.dot_general(
        a, b, (((0,), (0,)), ((), ())), precision=HIGHEST, preferred_element_type=F32
    )


def halves(x):
    h = x.astype(BF16)
    return h, (x - h.astype(F32)).astype(BF16)


def product4(a, b):
    k = b.shape[1]
    right = jnp.concatenate(halves(b), axis=1)
    both = jnp.dot(
        jnp.concatenate(halves(a), axis=1),
        jnp.concatenate([right, right], axis=0),
        preferred_element_type=F32,
    )
    return both[:, :k] + both[:, k:]


def product6(a, b):
    return jnp.dot(a, b, precision=HIGHEST, preferred_element_type=F32)


def shifted_inverses(grams):
    k = grams[0].shape[0]
    eye = lax.broadcasted_iota(jnp.int32, (k, k), 0) == lax.broadcasted_iota(
        jnp.int32, (k, k), 1
    )
    one = jnp.where(eye, 1.0, 0.0)
    low = 1.0 / (k / RIDGE + 1.0)
    gap = (1.0 - low) / (1.0 + low)
    first = 2.0 / (1.0 + low)
    tops, mats = [], []
    for gram in grams:
        trace = jnp.sum(jnp.where(eye, gram, 0.0), axis=(0, 1), keepdims=True)
        shift = RIDGE * (trace / k + 1e-06)
        tops.append(trace + shift)
        mats.append((gram + shift * one) / (trace + shift))
    scale = 2.0 / (2.0 - gap * gap)
    xs = [scale * (2.0 * first * one - first * first * m) for m in mats]
    gap = gap * gap / (2.0 - gap * gap)
    scales = []
    while gap > 2e-6:
        scales.append(2.0 / (2.0 - gap * gap))
        gap = gap * gap / (2.0 - gap * gap)
    pairs = [jnp.concatenate([product4(m, x), x], axis=0) for m, x in zip(mats, xs)]
    for scale in scales[:-1]:
        ys = [scale * (2.0 * one - pair[:k]) for pair in pairs]
        pairs = [product4(pair, y) for pair, y in zip(pairs, ys)]
    xs = [pair[k:] for pair in pairs]
    for scale in scales[-1:]:
        ys = [scale * (2.0 * one - product6(m, x)) for m, x in zip(mats, xs)]
        xs = [product4(x, y) for x, y in zip(xs, ys)]
    return [x / t for x, t in zip(xs, tops)]


def solve_kernel(
    rest_ref, g_ref, base_ref, place_ref, i1, i2, i3, top, o0, o1, o2, o3, root
):
    for got, o in ((i1, o1), (i2, o2), (i3, o3), (top, root)):
        o[...] = got[...]
    g, g_low = halves(g_ref[...])
    rest, rest_low = halves(rest_ref[...])
    dot = functools.partial(jnp.dot, preferred_element_type=F32)
    rows = dot(g, rest) + (dot(g, rest_low) + dot(g_low, rest))
    moved = lax.dot_general(
        place_ref[...], jnp.concatenate(halves(rows), axis=0), (((1,), (1,)), ((), ())),
        preferred_element_type=F32,
    )
    k = o0.shape[1]
    o0[...] = base_ref[...] + (moved[:, :k] + moved[:, k:])


def body(rows, cols, targets, sources, omega, tree_order, leaf_pivots, p1, p2, p3):
    n = rows * cols
    zs = cols // 2
    leaf = tree_order.shape[0]
    width = omega.shape[0]
    k = leaf_pivots.shape[1]
    rest = leaf - k
    spans = targets.shape[1] // LANES
    vmem = pl.BlockSpec(memory_space=pltpu.VMEM)
    hbm = pl.BlockSpec(memory_space=pltpu.HBM)
    dma = lambda *d: pltpu.SemaphoreType.DMA(d)
    held = lambda a: pltpu.VMEM(a.shape, a.dtype)
    order = tree_order.reshape(1, leaf)

    def stream(size):
        wide, narrow = (pltpu.VMEM((zs, width, size), t) for t in (F32, BF16))
        return [wide, wide, wide, narrow, narrow] + [dma(zs)] * 4

    out_rows = [leaf] + [k // 2**s for s in range(LEVELS)]
    kept = pl.pallas_call(
        functools.partial(sketch_kernel, rows, cols),
        out_shape=(
            pltpu.VMEM((width, rest), F32),
            pltpu.VMEM((k, width), F32),
            pltpu.VMEM((leaf, k), F32),
            pltpu.VMEM((leaf, rest), BF16),
        )
        + tuple(pltpu.VMEM((r, k), F32) for r in out_rows[1:])
        + (pltpu.VMEM((k // 2**LEVELS, width), F32),),
        in_specs=[hbm] * 8,
        out_specs=(vmem,) * (LEVELS + 5),
        scratch_shapes=[
            held(sources), held(omega), held(order), held(leaf_pivots),
            held(p1), held(p2), held(p3),
            pltpu.VMEM((n, 2, targets.shape[1]), F32),
            pltpu.VMEM((cols, 1, leaf), jnp.int32),
            pltpu.VMEM((2 * LANES, 2 * n * spans), BF16),
            pltpu.VMEM((sources.shape[1], SIDE), BF16),
            pltpu.VMEM((LEVELS + 1, width, k), F32),
            pltpu.VMEM((LEVELS, k, k), F32),
            pltpu.VMEM((k, width), F32),
            *stream(k), *stream(LANES), *stream(rest - LANES),
            pltpu.VMEM((width, k), F32),
            pltpu.VMEM((width, k), F32),
            pltpu.VMEM((width, k), BF16),
            pltpu.VMEM((GROUP - 1, width, k), BF16),
            dma(8),
            *[pltpu.SemaphoreType.DMA] * 6,
            *[dma(GROUP - 1)] * 4,
        ],
        compiler_params=pltpu.CompilerParams(
            collective_id=0, has_side_effects=True, vmem_limit_bytes=60 << 20
        ),
    )(targets, sources, omega, order, leaf_pivots, p1, p2, p3)
    return pl.pallas_call(
        solve_kernel,
        out_shape=tuple(jax.ShapeDtypeStruct((r, k), F32) for r in out_rows)
        + (jax.ShapeDtypeStruct((k // 2**LEVELS, width), F32),),
        in_specs=[vmem] * len(kept),
        out_specs=(vmem,) * (len(out_rows) + 1),
        compiler_params=pltpu.CompilerParams(vmem_limit_bytes=32 << 20),
    )(*kept)


def solution(mesh):
    both = P(("row", "col"), None)
    return jax.shard_map(
        functools.partial(body, mesh.shape["row"], mesh.shape["col"]),
        mesh=mesh,
        in_specs=(
            P(None, ("row", "col")),
            P(None, "col"),
            P(None, "col"),
            P(("row", "col")),
            both,
            P(),
            P(),
            P(),
        ),
        out_specs=(both,) * 5,
        check_vma=False,
    )
```
